32 devices in a mesh: groups: 2 (over y), seq: 4 (over z), mp: 2 (over x), rep: 2 (over core).
Axes of the slice: x: 2, y: 2, z: 4, core: 2. Of those that a mesh axis runs over, the one named last changes fastest.
Arguments:
- tokens: bfloat16 [8192, 2240], P(('groups', 'seq', 'rep')), parts along dimension 0, may hold values from -8 to 8
- slot_image: int32 [32], P(('groups', 'seq', 'rep')), parts along dimension 0, may hold values from 0 to 5, as said below
- modulation: float32 [12, 3, 2240], P('groups'), parts along dimension 0, may hold values from -3 to 3
- w_qkv: bfloat16 [2240, 3, 1280], P('rep', None, 'mp'), may hold values from -0.125 to 0.125
- w_out: bfloat16 [1280, 2240], P('rep', 'mp'), may hold values from -0.15625 to 0.15625
Outputs:
- updated: bfloat16 [8192, 2240], P(('groups', 'seq', 'rep'), 'mp'), parts along dimension 0
The draws below stay inside these ranges and needn't reach their ends.
There are 2 independent parts, one for each index of `groups`. The reference program is written for one: setup_inputs(seed, part) draws one part's arguments, and reference() takes and returns one part's arrays. A program takes and returns all parts, laid end to end along the dimension named above; an argument that names none is the same for every part. Nothing has to cross between parts.
Inputs may be any that keep to these rules, and one draw needn't show every extreme that they name: `slot_image`: every one of the 6 images owns one tile slot or more.
All inputs are finite; a program needn't handle non-finite values.
Results may differ from the reference program's by a relative error of at most 0.0036.
Values may be sent and summed in bfloat16 or wider, within the bound.
No kernel may reach another device: no remote copies, remote signals or barrier semaphores. Data moves between devices by JAX's collectives and lax.ppermute only.
A program may use at most 128 MiB of HBM per device.

```python
import math
import jax
import jax.numpy as jnp
from jax import lax

D = 2240
HD = 32
HEADS = 40
TILE = 256
IMAGES = 6
SLOTS = 16
TOKENS = 4096


def slot_images(key):
    folded = jax.random.fold_in(key, 11)
    first, second = jax.random.split(folded)
    extra = jax.random.randint(first, (SLOTS - IMAGES,), 0, IMAGES).astype(jnp.int32)
    listed = jnp.concatenate([jnp.arange(IMAGES, dtype=jnp.int32), extra])
    return jax.random.permutation(second, listed).astype(jnp.int32)


def draw_slot_image(key, part):
    return slot_images(key)


def draw_tokens(key, part):
    owners = slot_images(key)
    folded = jax.random.fold_in(key, 23)
    key_mean, key_offset, key_scale, key_noise, key_factor, key_loading = jax.random.split(folded, 6)
    means = jax.random.normal(key_mean, (IMAGES, D), jnp.float32) * 0.7
    offsets = jax.random.normal(key_offset, (SLOTS, D), jnp.float32) * 0.5
    scales = jnp.exp(jax.random.uniform(key_scale, (SLOTS, 1, 1), jnp.float32, math.log(0.3), math.log(2.5)))
    factors = jax.random.normal(key_factor, (SLOTS, TILE, 8), jnp.float32)
    loadings = jax.random.normal(key_loading, (SLOTS, 8, D), jnp.float32) * 0.3
    noise = jax.random.normal(key_noise, (SLOTS, TILE, D), jnp.float32)
    latent = factors[:, :, 0:1] * loadings[:, 0:1, :]
    for index in range(1, 8):
        latent = latent + factors[:, :, index:index + 1] * loadings[:, index:index + 1, :]
    centers = means[owners] + offsets
    values = centers[:, None, :] + scales * (noise + latent)
    return jnp.clip(values, -8.0, 8.0).reshape(SLOTS * TILE, D).astype(jnp.bfloat16)


def block_scale(stream_key, shape, pieces, least, largest):
    gain, own = 1.0, jax.random.fold_in(stream_key, 6)
    for position, blocks in pieces:
        heights = jnp.exp(jax.random.uniform(jax.random.fold_in(own, position), (blocks,), jnp.float32, least / len(pieces), largest / len(pieces)))
        gain = gain * jnp.repeat(heights, shape[position] // blocks).reshape([-1 if axis == position else 1 for axis in range(len(shape))])
    return gain


def bell_draw(stream_key, extent, deviation, bound, cuts=(), held_as=jnp.bfloat16):
    gain = block_scale(stream_key, extent, cuts, -0.22, 0.18) if cuts else 1.0
    array = jax.random.normal(stream_key, extent, jnp.float32) * deviation * gain
    return jnp.minimum(jnp.maximum(array, -bound), bound).astype(held_as)


def setup_inputs(seed: int = 0, part: int = 0) -> dict:
    keys = jax.random.split(jax.random.key(seed), 6)
    own_keys = jax.random.split(jax.random.fold_in(keys[5], part), 6)
    tokens = draw_tokens(jax.random.fold_in(jax.random.fold_in(keys[5], part), 71), part)
    slot_image = draw_slot_image(jax.random.fold_in(jax.random.fold_in(keys[5], part), 71), part)
    modulation = bell_draw(own_keys[2], (IMAGES, 3, D), 1.0, 3.0, (), jnp.float32)
    w_qkv = bell_draw(keys[3], (D, 3, HEADS * HD), D ** -0.5, 0.125, ((0, 2), (2, 2)))
    w_out = bell_draw(keys[4], (HEADS * HD, D), (HEADS * HD) ** -0.5, 0.15625, ((0, 2), (1, 2)))
    return dict(tokens=tokens, slot_image=slot_image, modulation=modulation, w_qkv=w_qkv, w_out=w_out)


def reference(tokens, slot_image, modulation, w_qkv, w_out):
    hi = lax.Precision.HIGHEST
    picker = (slot_image[:, None] == jnp.arange(IMAGES, dtype=jnp.int32)[None, :]).astype(jnp.float32)
    per_tile = jnp.dot(picker, modulation.reshape(IMAGES, 3 * D), precision=hi).reshape(SLOTS, 3, D)
    xf = tokens.astype(jnp.float32).reshape(SLOTS, TILE, D)
    mean = lax.optimization_barrier(jnp.mean(xf, axis=2, keepdims=True))
    var = lax.optimization_barrier(jnp.mean((xf - mean) ** 2, axis=2, keepdims=True))
    normed = (xf - mean) / jnp.sqrt(var + 1e-06)
    modulated = (normed * (1.0 + per_tile[:, None, 1, :]) + per_tile[:, None, 0, :]).astype(jnp.bfloat16)
    qkv = jnp.dot(modulated.reshape(TOKENS, D), w_qkv.reshape(D, 3 * HEADS * HD), preferred_element_type=jnp.float32)
    qkv = qkv.reshape(SLOTS, TILE, 3, HEADS, HD)
    query = jax.nn.relu(qkv[:, :, 0]).astype(jnp.bfloat16).astype(jnp.float32)
    keyf = jax.nn.relu(qkv[:, :, 1]).astype(jnp.bfloat16).astype(jnp.float32)
    value = qkv[:, :, 2].astype(jnp.bfloat16).astype(jnp.float32)
    tile_state = jnp.einsum('slhe,slhf->shef', keyf, value, precision=hi)
    tile_ksum = lax.optimization_barrier(jnp.sum(keyf, axis=1))
    state = jnp.einsum('si,shef->ihef', picker, tile_state, precision=hi)
    ksum = jnp.einsum('si,she->ihe', picker, tile_ksum, precision=hi)
    own_state = jnp.einsum('si,ihef->shef', picker, state, precision=hi)
    own_ksum = jnp.einsum('si,ihe->she', picker, ksum, precision=hi)
    numer = jnp.einsum('slhe,shef->slhf', query, own_state, precision=hi)
    denom = jnp.einsum('slhe,she->slh', query, own_ksum, precision=hi) + 1e-06
    attn = (numer / denom[..., None]).astype(jnp.bfloat16).reshape(TOKENS, HEADS * HD)
    projected = jnp.dot(attn, w_out, preferred_element_type=jnp.float32).reshape(SLOTS, TILE, D)
    updated = xf + per_tile[:, None, 2, :] * projected
    return updated.astype(jnp.bfloat16).reshape(TOKENS, D)
```

```python
import functools

import jax
import jax.numpy as jnp
from jax import lax
from jax.experimental import pallas as pl
from jax.experimental.pallas import tpu as pltpu
from jax.sharding import PartitionSpec as P

HD = 32
F32 = jnp.float32
BF16 = jnp.bfloat16
VM = pl.BlockSpec(memory_space=pltpu.VMEM)
HB = pl.BlockSpec(memory_space=pltpu.HBM)
MIB = 1 << 20


def call(kernel, name, out_shape, in_specs, out_specs=None, scratch=(), vmem=16, flops=0, nbytes=0):
    if out_specs is None:
        out_specs = [VM] * len(out_shape) if isinstance(out_shape, list) else VM
    return pl.pallas_call(
        kernel,
        out_shape=out_shape,
        in_specs=in_specs,
        out_specs=out_specs,
        scratch_shapes=list(scratch),
        compiler_params=pltpu.CompilerParams(vmem_limit_bytes=vmem * MIB),
        cost_estimate=pl.CostEstimate(flops=flops, bytes_accessed=nbytes, transcendentals=0),
        name=name,
    )


def load_kernel(w_ref, kv_ref, sems):
    count = kv_ref.shape[0]
    copies = [
        pltpu.make_async_copy(w_ref.at[c + 1], kv_ref.at[c], sems.at[c]) for c in range(count)
    ]
    for copy in copies:
        copy.start()
    for copy in copies:
        copy.wait()


def first_kernel(
    img_ref, x_ref, mods_ref, w_ref, kv_ref, mod_ref, part_ref, wq_ref, x_scr, mods_scr, img_scr,
    own_scr, sems,
):
    mine = lax.axis_index("rep")
    rows, half = mod_ref.shape
    width_in = x_ref.shape[0]
    halves = width_in // half
    tiles = img_ref.shape[0]
    step = 128
    per_tile = rows // tiles
    steps = rows // step
    img_copy = pltpu.make_async_copy(img_ref, img_scr, sems.at[0])
    mods_copy = pltpu.make_async_copy(mods_ref, mods_scr, sems.at[1])
    wq_copy = pltpu.make_async_copy(w_ref.at[0], wq_ref, sems.at[2])
    x_copies = [
        pltpu.make_async_copy(
            x_ref.at[:, pl.ds(i * step, step)], x_scr.at[:, pl.ds(i * step, step)], sems.at[3 + i]
        )
        for i in range(steps)
    ]
    img_copy.start()
    mods_copy.start()
    for copy in x_copies:
        copy.start()
    wq_copy.start()
    img_copy.wait()
    mods_copy.wait()
    for i in range(steps):
        x_copies[i].wait()
        at = slice(i * step, (i + 1) * step)
        parts = [
            x_scr[h * half : (h + 1) * half, at].astype(F32).T for h in range(halves)
        ]
        mean = sum(jnp.sum(p, axis=1, keepdims=True) for p in parts) / width_in
        parts = [p - mean for p in parts]
        var = sum(jnp.sum(p * p, axis=1, keepdims=True) for p in parts) / width_in
        inv = 1.0 / jnp.sqrt(var + 1e-06)
        mods = mods_scr[img_scr[i * step // per_tile]]
        for h in range(halves):
            shift = mods[0:1, h * half : (h + 1) * half]
            scale = mods[1:2, h * half : (h + 1) * half]
            own_scr[h, at, :] = (parts[h] * inv * (1.0 + scale) + shift).astype(BF16)
    mod_ref[...] = own_scr[1 - mine]
    for c in range(kv_ref.shape[0]):
        part_ref[c + 1] = jnp.dot(own_scr[mine], kv_ref[c], preferred_element_type=F32)
    wq_copy.wait()
    part_ref[0] = jnp.dot(own_scr[mine], wq_ref[...], preferred_element_type=F32)


def head_blocks(width):
    return [(start, min(128, width - start)) for start in range(0, width, 128)]


def same_head(rows, cols):
    return (
        lax.broadcasted_iota(jnp.int32, (rows, cols), 0) // HD
        == lax.broadcasted_iota(jnp.int32, (rows, cols), 1) // HD
    )


def state_rows(tiles):
    return tiles * HD + 8


def second_kernel(img_ref, mod_ref, w_ref, part_ref, state_ref, k_scr, v_scr, img_scr, sem):
    rows, width = k_scr.shape
    tiles = img_ref.shape[0]
    per_tile = rows // tiles
    img_copy = pltpu.make_async_copy(img_ref, img_scr, sem)
    img_copy.start()
    mod = mod_ref[...]
    k_scr[...] = jnp.maximum(
        part_ref[1] + jnp.dot(mod, w_ref[0], preferred_element_type=F32), 0.0
    ).astype(BF16)
    v_scr[...] = (
        part_ref[2] + jnp.dot(mod, w_ref[1], preferred_element_type=F32)
    ).astype(BF16)
    img_copy.wait()
    sums, images = [], []
    for t in range(tiles):
        span = slice(t * per_tile, (t + 1) * per_tile)
        sums.append(jnp.sum(k_scr[span, :].astype(F32), axis=0, keepdims=True))
        images.append(jnp.full((1, width), img_scr[t].astype(F32), F32))
        for start, size in head_blocks(width):
            full = lax.dot_general(
                v_scr[span, start : start + size],
                k_scr[span, start : start + size],
                (((0,), (0,)), ((), ())),
                preferred_element_type=F32,
            )
            full = jnp.where(same_head(size, size), full, 0.0)
            state_ref[t * HD : (t + 1) * HD, start : start + size] = sum(
                full[j * HD : (j + 1) * HD, :] for j in range(size // HD)
            ).astype(BF16)
    state_ref[tiles * HD :, :] = tail_rows(sums, images).astype(BF16)


def tail_rows(sums, images):
    rest = [s - s.astype(BF16).astype(F32) for s in sums]
    rows = sums + rest + images
    rows.append(jnp.zeros((8 - len(rows), sums[0].shape[1]), F32))
    return jnp.concatenate(rows, axis=0)


def query_kernel(mod_ref, w_ref, part_ref, after_ref, q_ref):
    q_ref[...] = jnp.maximum(
        part_ref[0] + jnp.dot(mod_ref[...], w_ref[...], preferred_element_type=F32), 0.0
    ).astype(BF16)


def sum_kernel(*refs):
    blocks, wide_ref, out_ref = refs[:-2], refs[-2], refs[-1]
    width = out_ref.shape[1]
    tiles = (out_ref.shape[0] - 8) // HD
    want = blocks[0][tiles * HD :, :].astype(F32)[2 * tiles : 3 * tiles]
    totals = [jnp.zeros((HD, width), F32)] * tiles
    sums = [jnp.zeros((1, width), F32)] * tiles
    for ref in blocks:
        tail = ref[tiles * HD :, :].astype(F32)
        for s in range(tiles):
            state = ref[s * HD : (s + 1) * HD, :].astype(F32)
            ksum = tail[s : s + 1] + tail[tiles + s : tiles + s + 1]
            for t in range(tiles):
                keep = (tail[2 * tiles + s : 2 * tiles + s + 1] == want[t : t + 1]).astype(F32)
                totals[t] += keep * state
                sums[t] += keep * ksum
    for t in range(tiles):
        wide_ref[t * HD : (t + 1) * HD, :] = totals[t]
        out_ref[t * HD : (t + 1) * HD, :] = totals[t].astype(BF16)
    tail = tail_rows(sums, [])
    wide_ref[tiles * HD :, :] = tail
    out_ref[tiles * HD :, :] = tail.astype(BF16)


def attend(q_ref, state_ref, out_ref, tiles):
    rows, width = q_ref.shape
    per_tile = rows // tiles
    exact = state_ref.dtype == F32
    tail = state_ref[tiles * HD :, :].astype(F32)
    for t in range(tiles):
        span = slice(t * per_tile, (t + 1) * per_tile)
        for start, size in head_blocks(width):
            lanes = slice(start, start + size)
            mask = same_head(size, size)
            state = state_ref[t * HD : (t + 1) * HD, lanes].astype(F32)
            state = jnp.concatenate([state] * (size // HD), axis=0)
            parts = [jnp.where(mask, state, 0.0)]
            for row in (t, tiles + t):
                parts.append(jnp.where(mask, jnp.broadcast_to(tail[row : row + 1, lanes], (size, size)), 0.0))
            if exact:
                parts.append(parts[0] - parts[0].astype(BF16).astype(F32))
            left = jnp.concatenate(parts, axis=0).astype(BF16)
            both = lax.dot_general(
                left, q_ref[span, lanes], (((1,), (1,)), ((), ())), preferred_element_type=F32
            )
            numer = both[:size]
            if exact:
                numer += both[3 * size :]
            denom = both[size : 2 * size] + both[2 * size : 3 * size] + 1e-06
            out_ref[start : start + size, span] = (numer / denom).astype(BF16)


def fetch_weights(p, width, w_refs, w_scr, sem):
    mine = lax.axis_index("rep")
    subs = w_refs[0].shape[1] // width
    for source, ref in enumerate(w_refs):
        @pl.when((p // subs == mine) == (source == 0))
        def _():
            pltpu.make_async_copy(ref, w_scr, sem).start()

    def finish():
        pltpu.make_async_copy(w_refs[0], w_scr, sem).wait()
        weights = w_scr[...]
        chosen = weights[:, :width]
        for s in range(1, subs):
            chosen = jnp.where(p % subs == s, weights[:, s * width : (s + 1) * width], chosen)
        return chosen

    return finish


def fifth_kernel(
    img_ref, q_ref, state_ref, w0_ref, w1_ref, x_ref, mods_ref, base_ref, gate_ref,
    attn_scr, w_scr, x_scr, gates_scr, img_scr, sems,
):
    m = lax.axis_index("mp")
    cols, rows = base_ref.shape
    tiles = img_ref.shape[0]
    per_tile = rows // tiles
    finish = fetch_weights(m, q_ref.shape[1], (w0_ref, w1_ref), w_scr, sems.at[0])
    copies = [
        pltpu.make_async_copy(img_ref, img_scr, sems.at[1]),
        pltpu.make_async_copy(x_ref.at[pl.ds(m * cols, cols), :], x_scr, sems.at[2]),
        pltpu.make_async_copy(mods_ref, gates_scr, sems.at[3]),
    ]
    for copy in copies:
        copy.start()
    attend(q_ref, state_ref, attn_scr, tiles)
    weights = finish()
    for copy in copies:
        copy.wait()
    total = jnp.dot(weights, attn_scr[...], preferred_element_type=F32)
    for t in range(tiles):
        gates = gates_scr[img_scr[t]][2:3]
        gate = gates[:, :cols]
        for p in range(1, gates.shape[1] // cols):
            gate = jnp.where(m == p, gates[:, p * cols : (p + 1) * cols], gate)
        for start in range(0, cols, 128):
            size = min(128, cols - start)
            column = jnp.broadcast_to(gate[:, start : start + size], (128, size)).T
            gate_ref[start : start + size, t * 128 : (t + 1) * 128] = column
            for left in range(t * per_tile, (t + 1) * per_tile, 128):
                piece = (slice(start, start + size), slice(left, left + 128))
                base_ref[piece] = x_scr[piece].astype(F32) + column * total[piece]


def sixth_kernel(others, mp, tiles, *refs):
    q_refs, state_refs = refs[:others], refs[others : 2 * others]
    w0_ref, w1_ref, base_ref, gate_ref, out_ref, attn_scr, w_scr, sems = refs[2 * others :]
    m = lax.axis_index("mp")
    cols, rows = out_ref.shape
    per_tile = rows // tiles
    total = None
    for index in range(others):
        p = lax.rem(m + mp - 1 - index, mp)
        finish = fetch_weights(p, q_refs[index].shape[1], (w0_ref, w1_ref), w_scr, sems.at[index])
        attend(q_refs[index], state_refs[index], attn_scr, tiles)
        part = jnp.dot(finish(), attn_scr[...], preferred_element_type=F32)
        total = part if total is None else total + part
    for t in range(tiles):
        column = gate_ref[:, t * 128 : (t + 1) * 128]
        for left in range(t * per_tile, (t + 1) * per_tile, 128):
            piece = (slice(0, cols), slice(left, left + 128))
            out_ref[piece] = (base_ref[piece] + column * total[piece]).astype(BF16)


def body(tokens, slot_image, modulation, w_qkv, w_out, *, seq, mp):
    rows, depth = tokens.shape
    tiles = slot_image.shape[0]
    half, _, width = w_qkv.shape
    heads_half, cols = w_out.shape
    swap = [(0, 1), (1, 0)]
    shape = jax.ShapeDtypeStruct
    x = tokens.T
    w = jnp.transpose(w_qkv, (1, 0, 2))
    wo = w_out.T
    dma = pltpu.SemaphoreType.DMA
    images = modulation.shape[0]

    def shift(value, axis, size, by):
        return lax.ppermute(value, axis, [(i, (i + by) % size) for i in range(size)])

    def across(value):
        return lax.ppermute(value, "rep", swap)

    kv = call(load_kernel, "load", shape((2, half, width), BF16), [HB], scratch=[dma((2,))], vmem=54,
              nbytes=4 * half * width)(w)
    kv_theirs = across(kv)
    mod, part, wq = call(
        first_kernel, "first",
        [shape((rows, half), BF16), shape((3, rows, width), F32), shape((half, width), BF16)],
        [HB, HB, HB, HB, VM],
        scratch=[
            pltpu.VMEM((depth, rows), BF16), pltpu.VMEM(modulation.shape, F32), pltpu.SMEM((tiles,), jnp.int32),
            pltpu.VMEM((depth // half, rows, half), BF16), dma((3 + rows // 128,)),
        ],
        vmem=48, flops=2 * rows * half * 3 * width, nbytes=12 * MIB,
    )(slot_image, x, modulation, w, kv)
    wq_theirs = across(wq)
    block = (state_rows(tiles), width)
    state = call(
        second_kernel, "second", shape(block, BF16), [HB, VM, VM, VM],
        scratch=[pltpu.VMEM((rows, width), BF16)] * 2 + [pltpu.SMEM((tiles,), jnp.int32), dma],
        flops=2 * rows * half * 2 * width, nbytes=8 * MIB,
    )(slot_image, mod, kv_theirs, part)
    near = [state] + [shift(state, "seq", seq, d) for d in range(1, seq)]
    q = call(
        query_kernel, "query", shape((rows, width), BF16), [VM, VM, VM, VM],
        flops=2 * rows * half * width, nbytes=4 * MIB,
    )(mod, wq_theirs, part, state)
    q_theirs = [shift(q, "mp", mp, d) for d in range(1, mp)]
    wo_theirs = across(wo)
    far = [across(b) for b in near]
    wide, final = call(
        sum_kernel, "sum", [shape(block, F32), shape(block, BF16)], [VM] * (2 * seq), nbytes=MIB,
    )(*near, *far)
    finals = [shift(final, "mp", mp, d) for d in range(1, mp)]
    base, gate = call(
        fifth_kernel, "own", [shape((cols, rows), F32), shape((cols, tiles * 128), F32)],
        [HB, VM, VM, HB, HB, HB, HB],
        scratch=[
            pltpu.VMEM((width, rows), BF16), pltpu.VMEM((cols, heads_half), BF16), pltpu.VMEM((cols, rows), BF16),
            pltpu.VMEM(modulation.shape, F32), pltpu.SMEM((tiles,), jnp.int32), dma((4,)),
        ],
        flops=2 * rows * width * cols, nbytes=4 * MIB,
    )(slot_image, q, wide, wo, wo_theirs, x, modulation)
    out = call(
        functools.partial(sixth_kernel, mp - 1, mp, tiles), "others", shape((cols, rows), BF16),
        [VM] * (2 * (mp - 1)) + [HB, HB, VM, VM],
        scratch=[pltpu.VMEM((width, rows), BF16), pltpu.VMEM((cols, heads_half), BF16), dma((mp - 1,))],
        flops=2 * rows * width * cols, nbytes=4 * MIB,
    )(*q_theirs, *finals, wo, wo_theirs, base, gate)
    return out.T


def solution(mesh):
    sizes = dict(mesh.shape)
    return jax.shard_map(
        functools.partial(body, seq=sizes["seq"], mp=sizes["mp"]),
        mesh=mesh,
        in_specs=(
            P(("groups", "seq", "rep"), None),
            P(("groups", "seq", "rep")),
            P("groups", None, None),
            P("rep", None, "mp"),
            P("rep", "mp"),
        ),
        out_specs=P(("groups", "seq", "rep"), "mp"),
        check_vma=False,
    )
```

```python
import functools

import jax
import jax.numpy as jnp
from jax import lax
from jax.experimental import pallas as pl
from jax.experimental.pallas import tpu as pltpu
from jax.sharding import PartitionSpec as P

HD = 32
F32 = jnp.float32
BF16 = jnp.bfloat16
VM = pl.BlockSpec(memory_space=pltpu.VMEM)
HB = pl.BlockSpec(memory_space=pltpu.HBM)
MIB = 1 << 20


def call(kernel, out_shape, in_specs, out_specs=None, scratch=(), vmem=16, aliases=None, flops=0, nbytes=0):
    if out_specs is None:
        out_specs = [VM] * len(out_shape) if isinstance(out_shape, list) else VM
    return pl.pallas_call(
        kernel,
        out_shape=out_shape,
        in_specs=in_specs,
        out_specs=out_specs,
        scratch_shapes=list(scratch),
        input_output_aliases=aliases or {},
        compiler_params=pltpu.CompilerParams(vmem_limit_bytes=vmem * MIB),
        cost_estimate=pl.CostEstimate(flops=flops, bytes_accessed=nbytes, transcendentals=0),
    )


def load_kernel(w_ref, out_ref, sem):
    copy = pltpu.make_async_copy(w_ref.at[0, :, pl.ds(0, out_ref.shape[1])], out_ref, sem)
    copy.start()
    copy.wait()


def column_sum(ref, at, function):
    rows = ref.shape[0]
    total = jnp.zeros((8, 128), F32)
    for start in range(0, rows, 64):
        size = min(64, rows - start)
        value = function(ref[start : start + size, at].astype(F32))
        total += jnp.sum(value.reshape(size // 8, 8, value.shape[1]), axis=0)
    return jnp.sum(total, axis=0, keepdims=True)


def norm_kernel(begin, end, spans, img_ref, x_ref, mods_ref, w_ref, *refs):
    if begin:
        refs = refs[2:]
    own_ref, other_ref, load_ref, img_scr, sel_scr, sems = refs
    mine = lax.axis_index("rep")
    rows, half = own_ref.shape
    width_in = x_ref.shape[0]
    tiles = img_ref.shape[0]
    step = 128
    per_tile = rows // tiles
    img_copy = pltpu.make_async_copy(img_ref, img_scr, sems.at[0])
    img_copy.start()
    copies = [
        pltpu.make_async_copy(
            w_ref.at[plane, :, pl.ds(start, size)], load_ref.at[at, :, pl.ds(left, size)], sems.at[1 + i]
        )
        for i, (plane, start, size, at, left) in enumerate(spans)
    ]
    for copy in copies:
        copy.start()
    img_copy.wait()
    for t in range(begin // per_tile, (end - 1) // per_tile + 1):
        mods = mods_ref[img_scr[t]]
        for row in range(2):
            low, high = mods[row : row + 1, :half], mods[row : row + 1, half:]
            if row:
                low, high = 1.0 + low, 1.0 + high
            sel_scr[t, row : row + 1] = jnp.where(mine == 0, low, high)
            sel_scr[t, 2 + row : 3 + row] = jnp.where(mine == 0, high, low)
    for start in range(begin, end, step):
        at = slice(start, start + step)
        t = start // per_tile
        mean = column_sum(x_ref, at, lambda v: v) / width_in
        var = column_sum(x_ref, at, lambda v: (v - mean) ** 2) / width_in
        inv = 1.0 / jnp.sqrt(var + 1e-06)
        mean = jnp.broadcast_to(mean, (step, step)).T
        inv = jnp.broadcast_to(inv, (step, step)).T
        for which, out in enumerate((own_ref, other_ref)):
            base = (mine if which == 0 else 1 - mine) * half
            for left in range(0, half, step):
                size = min(step, half - left)
                first = pl.multiple_of(base + left, 16)
                value = x_ref[pl.ds(first, size), at].T.astype(F32)
                lanes = slice(left, left + size)
                shift = sel_scr[t, 2 * which : 2 * which + 1, lanes]
                scale = sel_scr[t, 2 * which + 1 : 2 * which + 2, lanes]
                out[at, lanes] = (
                    (value - mean[:, :size]) * inv[:, :size] * scale + shift
                ).astype(BF16)
    for copy in copies:
        copy.wait()


def query_kernel(own_ref, other_ref, w_ref, w_other_ref, q_ref):
    total = jnp.dot(own_ref[...], w_ref[...], preferred_element_type=F32)
    total += jnp.dot(other_ref[...], w_other_ref[...], preferred_element_type=F32)
    q_ref[...] = jnp.maximum(total, 0.0).astype(BF16)


def part_kernel(own_ref, w_ref, after_ref, part_ref):
    for c in range(part_ref.shape[0]):
        part_ref[c] = jnp.dot(own_ref[...], w_ref[c], preferred_element_type=F32)


def head_blocks(width):
    return [(start, min(128, width - start)) for start in range(0, width, 128)]


def same_head(rows, cols):
    return (
        lax.broadcasted_iota(jnp.int32, (rows, cols), 0) // HD
        == lax.broadcasted_iota(jnp.int32, (rows, cols), 1) // HD
    )


def state_rows(tiles):
    return tiles * HD + 8


def second_kernel(img_ref, mod_ref, w_ref, part_ref, state_ref, k_scr, v_scr, img_scr, sem):
    rows, width = k_scr.shape
    tiles = img_ref.shape[0]
    per_tile = rows // tiles
    img_copy = pltpu.make_async_copy(img_ref, img_scr, sem)
    img_copy.start()
    mod = mod_ref[...]
    for c in range(w_ref.shape[0]):
        total = part_ref[c] + jnp.dot(mod, w_ref[c], preferred_element_type=F32)
        if c == 0:
            k_scr[...] = jnp.maximum(total[:, :width], 0.0).astype(BF16)
        if c == w_ref.shape[0] - 1:
            v_scr[...] = total[:, total.shape[1] - width :].astype(BF16)
    img_copy.wait()
    sums, images = [], []
    for t in range(tiles):
        span = slice(t * per_tile, (t + 1) * per_tile)
        sums.append(jnp.sum(k_scr[span, :].astype(F32), axis=0, keepdims=True))
        images.append(jnp.full((1, width), img_scr[t].astype(F32), F32))
        for start, size in head_blocks(width):
            full = lax.dot_general(
                v_scr[span, start : start + size],
                k_scr[span, start : start + size],
                (((0,), (0,)), ((), ())),
                preferred_element_type=F32,
            )
            full = jnp.where(same_head(size, size), full, 0.0)
            state_ref[t * HD : (t + 1) * HD, start : start + size] = sum(
                full[j * HD : (j + 1) * HD, :] for j in range(size // HD)
            ).astype(BF16)
    state_ref[tiles * HD :, :] = tail_rows(sums, images).astype(BF16)


def tail_rows(sums, images):
    rest = [s - s.astype(BF16).astype(F32) for s in sums]
    rows = sums + rest + images
    rows.append(jnp.zeros((8 - len(rows), sums[0].shape[1]), F32))
    return jnp.concatenate(rows, axis=0)


def sum_kernel(*refs):
    blocks, wide_ref, out_ref = refs[:-2], refs[-2], refs[-1]
    width = out_ref.shape[1]
    tiles = (out_ref.shape[0] - 8) // HD
    want = blocks[0][tiles * HD :, :].astype(F32)[2 * tiles : 3 * tiles]
    totals = [jnp.zeros((HD, width), F32)] * tiles
    sums = [jnp.zeros((1, width), F32)] * tiles
    for ref in blocks:
        tail = ref[tiles * HD :, :].astype(F32)
        for s in range(tiles):
            state = ref[s * HD : (s + 1) * HD, :].astype(F32)
            ksum = tail[s : s + 1] + tail[tiles + s : tiles + s + 1]
            for t in range(tiles):
                keep = (tail[2 * tiles + s : 2 * tiles + s + 1] == want[t : t + 1]).astype(F32)
                totals[t] += keep * state
                sums[t] += keep * ksum
    for t in range(tiles):
        wide_ref[t * HD : (t + 1) * HD, :] = totals[t]
        out_ref[t * HD : (t + 1) * HD, :] = totals[t].astype(BF16)
    tail = tail_rows(sums, [])
    wide_ref[tiles * HD :, :] = tail
    out_ref[tiles * HD :, :] = tail.astype(BF16)


def attend(q_refs, state_ref, out_ref, tiles):
    width, rows = out_ref.shape
    per_tile = rows // tiles
    first = q_refs[0].shape[1]
    exact = state_ref.dtype == F32
    tail = state_ref[tiles * HD :, :].astype(F32)
    for t in range(tiles):
        span = slice(t * per_tile, (t + 1) * per_tile)
        for start, size in head_blocks(width):
            lanes = slice(start, start + size)
            mask = same_head(size, size)
            state = state_ref[t * HD : (t + 1) * HD, lanes].astype(F32)
            state = jnp.concatenate([state] * (size // HD), axis=0)
            parts = [jnp.where(mask, state, 0.0)]
            for row in (t, tiles + t):
                parts.append(jnp.where(mask, jnp.broadcast_to(tail[row : row + 1, lanes], (size, size)), 0.0))
            if exact:
                parts.append(parts[0] - parts[0].astype(BF16).astype(F32))
            left = jnp.concatenate(parts, axis=0).astype(BF16)
            both = lax.dot_general(
                left,
                q_refs[0][span, lanes] if start < first else q_refs[1][span, start - first : start - first + size],
                (((1,), (1,)), ((), ())), preferred_element_type=F32,
            )
            numer = both[:size]
            if exact:
                numer += both[3 * size :]
            denom = both[size : 2 * size] + both[2 * size : 3 * size] + 1e-06
            out_ref[start : start + size, span] = (numer / denom).astype(BF16)


def fetch_weights(p, width, w_refs, w_scr, sem):
    mine = lax.axis_index("rep")
    subs = w_refs[0].shape[1] // width
    for source, ref in enumerate(w_refs):
        @pl.when((p // subs == mine) == (source == 0))
        def _():
            pltpu.make_async_copy(ref, w_scr, sem).start()

    def finish():
        pltpu.make_async_copy(w_refs[0], w_scr, sem).wait()
        weights = w_scr[...]
        chosen = weights[:, :width]
        for s in range(1, subs):
            chosen = jnp.where(p % subs == s, weights[:, s * width : (s + 1) * width], chosen)
        return chosen

    return finish


def fifth_kernel(
    img_ref, qa_ref, qb_ref, state_ref, w0_ref, w1_ref, x_ref, mods_ref, base_ref, gate_ref,
    attn_scr, w_scr, x_scr, gates_scr, img_scr, sems,
):
    m = lax.axis_index("mp")
    cols, rows = base_ref.shape
    tiles = img_ref.shape[0]
    per_tile = rows // tiles
    finish = fetch_weights(m, attn_scr.shape[0], (w0_ref, w1_ref), w_scr, sems.at[0])
    copies = [
        pltpu.make_async_copy(img_ref, img_scr, sems.at[1]),
        pltpu.make_async_copy(x_ref.at[pl.ds(m * cols, cols), :], x_scr, sems.at[2]),
        pltpu.make_async_copy(mods_ref, gates_scr, sems.at[3]),
    ]
    for copy in copies:
        copy.start()
    attend((qa_ref, qb_ref), state_ref, attn_scr, tiles)
    weights = finish()
    for copy in copies:
        copy.wait()
    total = jnp.dot(weights, attn_scr[...], preferred_element_type=F32)
    for t in range(tiles):
        gates = gates_scr[img_scr[t]][2:3]
        gate = gates[:, :cols]
        for p in range(1, gates.shape[1] // cols):
            gate = jnp.where(m == p, gates[:, p * cols : (p + 1) * cols], gate)
        for start in range(0, cols, 128):
            size = min(128, cols - start)
            column = jnp.broadcast_to(gate[:, start : start + size], (128, size)).T
            gate_ref[start : start + size, t * 128 : (t + 1) * 128] = column
            for left in range(t * per_tile, (t + 1) * per_tile, 128):
                piece = (slice(start, start + size), slice(left, left + 128))
                base_ref[piece] = x_scr[piece].astype(F32) + column * total[piece]


def sixth_kernel(others, mp, tiles, *refs):
    qa_refs, qb_refs, state_refs = (refs[i * others : (i + 1) * others] for i in range(3))
    w0_ref, w1_ref, base_ref, gate_ref, out_ref, attn_scr, out_scr, sems = refs[3 * others :]
    m, mine = lax.axis_index("mp"), lax.axis_index("rep")
    cols, rows = out_ref.shape
    per_tile = rows // tiles
    width = attn_scr.shape[0]
    subs = w0_ref.shape[1] // width
    for index in range(others):
        attend((qa_refs[index], qb_refs[index]), state_refs[index], attn_scr, tiles)
        p = lax.rem(m + mp - 1 - index, mp)
        last = index == others - 1
        for source, ref in enumerate((w0_ref, w1_ref)):
            for s in range(subs):
                here = jnp.logical_and((p // subs == mine) == (source == 0), p % subs == s)

                @pl.when(here)
                def _(ref=ref, s=s, last=last):
                    for number, (start, size) in enumerate(pieces(cols)):
                        span = slice(start, start + size)
                        part = jnp.dot(
                            ref[span, s * width : (s + 1) * width], attn_scr[...],
                            preferred_element_type=F32,
                        )
                        for t in range(tiles):
                            column = gate_ref[span, t * 128 : (t + 1) * 128]
                            for left in range(t * per_tile, (t + 1) * per_tile, 128):
                                lanes = slice(left, left + 128)
                                value = base_ref[span, lanes] + column * part[:, lanes]
                                if last:
                                    out_scr[span, lanes] = value.astype(BF16)
                                else:
                                    base_ref[span, lanes] = value
                        if last:
                            pltpu.make_async_copy(
                                out_scr.at[span], out_ref.at[span], sems.at[number]
                            ).start()
    for number, (start, size) in enumerate(pieces(cols)):
        span = slice(start, start + size)
        pltpu.make_async_copy(out_scr.at[span], out_ref.at[span], sems.at[number]).wait()


def pieces(cols):
    unit = cols // 16 // 4 * 16
    return [(0, cols - 2 * unit), (cols - 2 * unit, unit), (cols - unit, unit)]


def seq_order(seq):
    return [*range((seq + 1) // 2, seq), *range(1, (seq + 1) // 2)]


def body(tokens, slot_image, modulation, w_qkv, w_out, *, seq, mp):
    rows, depth = tokens.shape
    tiles = slot_image.shape[0]
    half, _, width = w_qkv.shape
    heads_half, cols = w_out.shape
    swap = [(0, 1), (1, 0)]
    in_hbm = functools.partial(pltpu.with_memory_space_constraint, memory_space=pltpu.HBM)
    shape = jax.ShapeDtypeStruct
    x = in_hbm(tokens.T)
    w = in_hbm(jnp.transpose(w_qkv, (1, 0, 2)))
    wo = w_out.T
    dma = pltpu.SemaphoreType.DMA

    def shift(value, axis, size, by):
        return lax.ppermute(value, axis, [(i, (i + by) % size) for i in range(size)])

    def swap_seq(value, d):
        if seq & (seq - 1):
            return shift(value, "seq", seq, d)
        return lax.ppermute(value, "seq", [(i, i ^ d) for i in range(seq)])

    def across(value):
        return lax.ppermute(value, "rep", swap)

    lead = min(256, width // 256 * 128)
    wa = call(
        load_kernel, shape((half, lead), BF16), [HB], scratch=[dma], vmem=4,
        nbytes=2 * half * lead,
    )(w)
    wa_theirs = across(wa)
    joined = width % 128 == 0
    kv_shape = (1, half, 2 * width) if joined else (2, half, width)
    kv_spans = [
        (1 + c, 0, width, 0 if joined else c, c * width if joined else 0) for c in range(2)
    ]

    def norm(begin, end, spans, loaded, *before):
        return call(
            functools.partial(norm_kernel, begin, end, spans),
            [shape((rows, half), BF16)] * 2 + [shape(loaded, BF16)],
            [HB, VM, VM, HB] + [VM] * len(before),
            scratch=[pltpu.SMEM((tiles,), jnp.int32), pltpu.VMEM((tiles, 8, half), F32), dma((1 + len(spans),))],
            aliases={4 + i: i for i in range(len(before))}, nbytes=4 * MIB,
        )(slot_image, tokens.T, modulation, w, *before)

    split = rows // 256 * 128
    own, other, kv = norm(0, split, kv_spans, kv_shape)
    kv_theirs = across(kv)
    own, other, wb = norm(
        split, rows, [(0, lead, width - lead, 0, 0)], (1, half, width - lead), own, other
    )
    wb_theirs = across(wb)

    def query(size, mine, theirs):
        return call(
            query_kernel, shape((rows, size), BF16), [VM] * 4,
            flops=2 * rows * depth * size, nbytes=3 * MIB,
        )(own, other, mine, theirs)

    qa = query(lead, wa, wa_theirs)
    qa_theirs = [shift(qa, "mp", mp, d) for d in range(1, mp)]
    part = call(
        part_kernel, shape((kv_shape[0], rows, kv_shape[2]), F32), [VM] * 3,
        flops=2 * rows * half * 2 * width, nbytes=4 * MIB,
    )(own, kv, qa)
    block = (state_rows(tiles), width)
    state = call(
        second_kernel, shape(block, BF16), [HB, VM, VM, VM],
        scratch=[pltpu.VMEM((rows, width), BF16)] * 2 + [pltpu.SMEM((tiles,), jnp.int32), dma],
        flops=2 * rows * half * 2 * width, nbytes=8 * MIB,
    )(slot_image, other, kv_theirs, part)
    near = [state] + [swap_seq(state, d) for d in seq_order(seq)]
    qb = query(width - lead, wb[0], wb_theirs[0])
    qb_theirs = [shift(qb, "mp", mp, d) for d in range(1, mp)]
    wo_theirs = across(wo)
    far = [across(b) for b in near]
    wide, final = call(
        sum_kernel, [shape(block, F32), shape(block, BF16)], [VM] * (2 * seq), nbytes=MIB,
    )(*near, *far)
    finals = [shift(final, "mp", mp, d) for d in range(1, mp)]
    base, gate = call(
        fifth_kernel, [shape((cols, rows), F32), shape((cols, tiles * 128), F32)],
        [HB, VM, VM, VM, HB, HB, HB, HB],
        scratch=[
            pltpu.VMEM((width, rows), BF16), pltpu.VMEM((cols, heads_half), BF16), pltpu.VMEM((cols, rows), BF16),
            pltpu.VMEM(modulation.shape, F32), pltpu.SMEM((tiles,), jnp.int32), dma((4,)),
        ],
        flops=2 * rows * width * cols, nbytes=4 * MIB,
    )(slot_image, qa, qb, wide, wo, wo_theirs, x, modulation)
    out = call(
        functools.partial(sixth_kernel, mp - 1, mp, tiles), shape((cols, rows), BF16),
        [VM] * (3 * (mp - 1) + 4), out_specs=HB,
        scratch=[pltpu.VMEM((width, rows), BF16), pltpu.VMEM((cols, rows), BF16), dma((3,))],
        flops=2 * rows * width * cols, nbytes=4 * MIB,
    )(*qa_theirs, *qb_theirs, *finals, wo, wo_theirs, base, gate)
    return out.T


def solution(mesh):
    sizes = dict(mesh.shape)

    def step(*args):
        return body(*args, seq=sizes["seq"], mp=sizes["mp"])

    return jax.shard_map(
        step,
        mesh=mesh,
        in_specs=(
            P(("groups", "seq", "rep"), None),
            P(("groups", "seq", "rep")),
            P("groups", None, None),
            P("rep", None, "mp"),
            P("rep", "mp"),
        ),
        out_specs=P(("groups", "seq", "rep"), "mp"),
        check_vma=False,
    )
```

```python
import functools

import jax
import jax.numpy as jnp
from jax import lax
from jax.experimental import pallas as pl
from jax.experimental.pallas import tpu as pltpu
from jax.sharding import PartitionSpec as P

HD = 32
F32 = jnp.float32
BF16 = jnp.bfloat16
VM = pl.BlockSpec(memory_space=pltpu.VMEM)
HB = pl.BlockSpec(memory_space=pltpu.HBM)
MIB = 1 << 20


def call(kernel, out_shape, in_specs, out_specs=None, scratch=(), vmem=16, aliases=None, flops=0, nbytes=0):
    if out_specs is None:
        out_specs = [VM] * len(out_shape) if isinstance(out_shape, list) else VM
    return pl.pallas_call(
        kernel,
        out_shape=out_shape,
        in_specs=in_specs,
        out_specs=out_specs,
        scratch_shapes=list(scratch),
        input_output_aliases=aliases or {},
        compiler_params=pltpu.CompilerParams(vmem_limit_bytes=vmem * MIB),
        cost_estimate=pl.CostEstimate(flops=flops, bytes_accessed=nbytes, transcendentals=0),
    )


def column_sum(ref, at, function):
    rows = ref.shape[0]
    total = jnp.zeros((8, 128), F32)
    for start in range(0, rows, 64):
        size = min(64, rows - start)
        value = function(ref[start : start + size, at].astype(F32))
        total += jnp.sum(value.reshape(size // 8, 8, value.shape[1]), axis=0)
    return jnp.sum(total, axis=0, keepdims=True)


def norm_kernel(begin, end, spans, loaded, img_ref, x_ref, mods_ref, w_ref, *refs):
    known = refs[2:4] if begin else ()
    refs = refs[len(known) + 2 :] if begin else refs
    own_ref, other_ref = refs[:2]
    load_refs, refs = refs[2 : 2 + loaded], refs[2 + loaded :]
    part_refs = refs[: len(known)]
    img_scr, sel_scr, sems, *more = refs[len(known) :]
    mine = lax.axis_index("rep")
    rows, half = own_ref.shape
    width_in = x_ref.shape[0]
    tiles = img_ref.shape[0]
    step = 128
    per_tile = rows // tiles
    steps = (end - begin) // step
    early = [pltpu.make_async_copy(img_ref, img_scr, sems.at[0])]
    x_copies = [None] * steps
    copies = []
    if not begin:
        x_scr, mods_scr = more
        early.append(pltpu.make_async_copy(mods_ref, mods_scr, sems.at[1]))
        x_copies = [
            pltpu.make_async_copy(
                x_ref.at[:, pl.ds(i * step, step)], x_scr.at[:, pl.ds(i * step, step)], sems.at[3 + i]
            )
            for i in range(steps)
        ]
        copies.append(pltpu.make_async_copy(x_ref.at[:, pl.ds(end, rows - end)], load_refs[-1], sems.at[2]))
        for copy in x_copies[:1] + early + x_copies[1:]:
            copy.start()
        x_ref, mods_ref = x_scr, mods_scr
    else:
        early[0].start()
    copies = [
        pltpu.make_async_copy(
            w_ref.at[plane, :, pl.ds(start, size)], load_refs[out].at[at, :, pl.ds(left, size)],
            sems.at[3 + steps + i],
        )
        for i, (out, plane, start, size, at, left) in enumerate(spans)
    ] + copies
    for copy in copies:
        copy.start()
    products = product_list(own_ref, known, part_refs, slice(0, begin))
    total = steps * 2 * -(-half // step)
    count, done = 0, 0
    for index in range(steps):
        start = begin + index * step
        at = slice(start, start + step)
        t = start // per_tile
        x_at = slice(index * step, (index + 1) * step)
        if x_copies[index] is not None:
            x_copies[index].wait()
        mean = column_sum(x_ref, x_at, lambda v: v) / width_in
        var = column_sum(x_ref, x_at, lambda v: (v - mean) ** 2) / width_in
        inv = 1.0 / jnp.sqrt(var + 1e-06)
        mean = jnp.broadcast_to(mean, (step, step)).T
        inv = jnp.broadcast_to(inv, (step, step)).T
        if not index:
            for copy in early:
                copy.wait()
        if not index or start % per_tile == 0:
            mods = mods_ref[img_scr[t]]
            for row in range(2):
                low, high = mods[row : row + 1, :half], mods[row : row + 1, half:]
                if row:
                    low, high = 1.0 + low, 1.0 + high
                sel_scr[t, row : row + 1] = jnp.where(mine == 0, low, high)
                sel_scr[t, 2 + row : 3 + row] = jnp.where(mine == 0, high, low)
        for which, out in enumerate((own_ref, other_ref)):
            base = (mine if which == 0 else 1 - mine) * half
            for left in range(0, half, step):
                size = min(step, half - left)
                first = pl.multiple_of(base + left, 16)
                value = x_ref[pl.ds(first, size), x_at].T.astype(F32)
                lanes = slice(left, left + size)
                shift = sel_scr[t, 2 * which : 2 * which + 1, lanes]
                scale = sel_scr[t, 2 * which + 1 : 2 * which + 2, lanes]
                out[at, lanes] = (
                    (value - mean[:, :size]) * inv[:, :size] * scale + shift
                ).astype(BF16)
                count += 1
                while done * total < count * len(products):
                    products[done]()
                    done += 1
    for copy in copies:
        copy.wait()


def product_list(own_ref, w_refs, part_refs, rows):
    def product(w_ref, part_ref, c, lanes):
        part_ref[c, rows, lanes] = jnp.dot(
            own_ref[rows, :], w_ref[c, :, lanes], preferred_element_type=F32
        )

    return [
        functools.partial(product, w_ref, part_ref, c, slice(at, min(at + 256, w_ref.shape[2])))
        for w_ref, part_ref in zip(w_refs, part_refs)
        for c in range(w_ref.shape[0])
        for at in range(0, w_ref.shape[2], 256)
    ]


def query_kernel(own_ref, other_ref, w_ref, w_other_ref, q_ref):
    total = jnp.dot(own_ref[...], w_ref[...], preferred_element_type=F32)
    total += jnp.dot(other_ref[...], w_other_ref[...], preferred_element_type=F32)
    q_ref[...] = jnp.maximum(total, 0.0).astype(BF16)


def part_kernel(begin, own_ref, w0_ref, w1_ref, after_ref, *refs):
    outs = refs[-2:]
    for product in product_list(own_ref, (w0_ref, w1_ref), outs, slice(begin, own_ref.shape[0])):
        product()


def head_blocks(width):
    return [(start, min(128, width - start)) for start in range(0, width, 128)]


def same_head(rows, cols):
    return (
        lax.broadcasted_iota(jnp.int32, (rows, cols), 0) // HD
        == lax.broadcasted_iota(jnp.int32, (rows, cols), 1) // HD
    )


def state_rows(tiles):
    return tiles * HD + 8


def second_kernel(offset, img_ref, mod_ref, w_ref, part_ref, *refs):
    state_ref, k_scr, v_scr, img_scr, sem = refs[-5:]
    rows, width = k_scr.shape
    tiles = img_ref.shape[0]
    per_tile = rows // tiles
    img_copy = pltpu.make_async_copy(img_ref, img_scr, sem)
    img_copy.start()
    mod = mod_ref[...]
    for c in range(w_ref.shape[0]):
        total = part_ref[c] + jnp.dot(mod, w_ref[c], preferred_element_type=F32)
        if c == 0:
            k_scr[...] = jnp.maximum(total[:, :width], 0.0).astype(BF16)
        if c == w_ref.shape[0] - 1:
            v_scr[...] = total[:, total.shape[1] - width :].astype(BF16)
    img_copy.wait()
    sums, images = [], []
    for t in range(tiles):
        span = slice(t * per_tile, (t + 1) * per_tile)
        sums.append(jnp.sum(k_scr[span, :].astype(F32), axis=0, keepdims=True))
        images.append(jnp.full((1, width), img_scr[t].astype(F32), F32))
        for start, size in head_blocks(width):
            full = lax.dot_general(
                v_scr[span, start : start + size],
                k_scr[span, start : start + size],
                (((0,), (0,)), ((), ())),
                preferred_element_type=F32,
            )
            full = jnp.where(same_head(size, size), full, 0.0)
            state_ref[t * HD : (t + 1) * HD, offset + start : offset + start + size] = sum(
                full[j * HD : (j + 1) * HD, :] for j in range(size // HD)
            ).astype(BF16)
    state_ref[tiles * HD :, offset : offset + width] = tail_rows(sums, images).astype(BF16)


def tail_rows(sums, images):
    rest = [s - s.astype(BF16).astype(F32) for s in sums]
    rows = sums + rest + images
    rows.append(jnp.zeros((8 - len(rows), sums[0].shape[1]), F32))
    return jnp.concatenate(rows, axis=0)


def add_states(totals, sums, want, blocks, tiles):
    for ref in blocks:
        tail = ref[tiles * HD :, :].astype(F32)
        for s in range(tiles):
            state = ref[s * HD : (s + 1) * HD, :].astype(F32)
            ksum = tail[s : s + 1] + tail[tiles + s : tiles + s + 1]
            for t in range(tiles):
                keep = (tail[2 * tiles + s : 2 * tiles + s + 1] == want[t : t + 1]).astype(F32)
                totals[t] += keep * state
                sums[t] += keep * ksum


def wanted(ref, tiles):
    return ref[tiles * HD :, :].astype(F32)[2 * tiles : 3 * tiles]


def sum_kernel(*refs):
    blocks, wide_ref = refs[:-1], refs[-1]
    width = wide_ref.shape[1]
    tiles = (wide_ref.shape[0] - 8) // HD
    totals = [jnp.zeros((HD, width), F32)] * tiles
    sums = [jnp.zeros((1, width), F32)] * tiles
    add_states(totals, sums, wanted(blocks[0], tiles), blocks, tiles)
    for t in range(tiles):
        wide_ref[t * HD : (t + 1) * HD, :] = totals[t]
    wide_ref[tiles * HD :, :] = jnp.concatenate(
        sums + [jnp.zeros((8 - tiles, width), F32)], axis=0
    )


def last_kernel(own_ref, so_far_ref, block_ref, wide_ref, out_ref):
    tiles = (out_ref.shape[0] - 8) // HD
    totals = [so_far_ref[t * HD : (t + 1) * HD, :] for t in range(tiles)]
    known = so_far_ref[tiles * HD :, :]
    sums = [known[t : t + 1] for t in range(tiles)]
    add_states(totals, sums, wanted(own_ref, tiles), (block_ref,), tiles)
    for t in range(tiles):
        wide_ref[t * HD : (t + 1) * HD, :] = totals[t]
        out_ref[t * HD : (t + 1) * HD, :] = totals[t].astype(BF16)
    tail = tail_rows(sums, [])
    wide_ref[tiles * HD :, :] = tail
    out_ref[tiles * HD :, :] = tail.astype(BF16)


def attend(q_refs, state_ref, out_ref, tiles):
    width, rows = out_ref.shape
    per_tile = rows // tiles
    first = q_refs[0].shape[1]
    exact = state_ref.dtype == F32
    tail = state_ref[tiles * HD :, :].astype(F32)
    for t in range(tiles):
        span = slice(t * per_tile, (t + 1) * per_tile)
        for start, size in head_blocks(width):
            lanes = slice(start, start + size)
            mask = same_head(size, size)
            state = state_ref[t * HD : (t + 1) * HD, lanes].astype(F32)
            state = jnp.concatenate([state] * (size // HD), axis=0)
            heads = size // HD
            parts = [jnp.where(mask, state, 0.0)]
            if exact:
                parts.append(parts[0] - parts[0].astype(BF16).astype(F32))
            row = lax.broadcasted_iota(jnp.int32, (8, size), 0)
            head = lax.broadcasted_iota(jnp.int32, (8, size), 1) // HD
            sums = jnp.where(row < 4, tail[t : t + 1, lanes], tail[tiles + t : tiles + t + 1, lanes])
            parts.append(jnp.where(row % 4 == head, sums, 0.0))
            left = jnp.concatenate(parts, axis=0).astype(BF16)
            both = lax.dot_general(
                left,
                q_refs[0][span, lanes] if start < first else q_refs[1][span, start - first : start - first + size],
                (((1,), (1,)), ((), ())), preferred_element_type=F32,
            )
            numer = both[:size]
            if exact:
                numer += both[size : 2 * size]
            sums = both[-8:]
            inverse = 1.0 / (sums[:4] + sums[4:] + 1e-06)
            inverse = jnp.concatenate(
                [jnp.broadcast_to(inverse[j : j + 1], (HD, per_tile)) for j in range(heads)], axis=0
            )
            out_ref[start : start + size, span] = (numer * inverse).astype(BF16)


def fetch_weights(p, width, w_refs, w_scr, sem):
    mine = lax.axis_index("rep")
    subs = w_refs[0].shape[1] // width
    for source, ref in enumerate(w_refs):
        @pl.when((p // subs == mine) == (source == 0))
        def _():
            pltpu.make_async_copy(ref, w_scr, sem).start()

    def finish():
        pltpu.make_async_copy(w_refs[0], w_scr, sem).wait()
        weights = w_scr[...]
        chosen = weights[:, :width]
        for s in range(1, subs):
            chosen = jnp.where(p % subs == s, weights[:, s * width : (s + 1) * width], chosen)
        return chosen

    return finish


def fifth_kernel(
    img_ref, qa_ref, qb_ref, state_ref, w0_ref, w1_ref, x_ref, mods_ref, base_ref, gate_ref,
    attn_scr, w_scr, x_scr, gates_scr, img_scr, sems,
):
    m = lax.axis_index("mp")
    cols, rows = base_ref.shape
    tiles = img_ref.shape[0]
    per_tile = rows // tiles
    finish = fetch_weights(m, attn_scr.shape[0], (w0_ref, w1_ref), w_scr, sems.at[0])
    copies = [
        pltpu.make_async_copy(img_ref, img_scr, sems.at[1]),
        pltpu.make_async_copy(x_ref.at[pl.ds(m * cols, cols), :], x_scr, sems.at[2]),
        pltpu.make_async_copy(mods_ref, gates_scr, sems.at[3]),
    ]
    for copy in copies:
        copy.start()
    attend((qa_ref, qb_ref), state_ref, attn_scr, tiles)
    weights = finish()
    for copy in copies:
        copy.wait()
    total = jnp.dot(weights, attn_scr[...], preferred_element_type=F32)
    for t in range(tiles):
        gates = gates_scr[img_scr[t]][2:3]
        gate = gates[:, :cols]
        for p in range(1, gates.shape[1] // cols):
            gate = jnp.where(m == p, gates[:, p * cols : (p + 1) * cols], gate)
        for start in range(0, cols, 128):
            size = min(128, cols - start)
            column = jnp.broadcast_to(gate[:, start : start + size], (128, size)).T
            gate_ref[start : start + size, t * 128 : (t + 1) * 128] = column
            for left in range(t * per_tile, (t + 1) * per_tile, 128):
                piece = (slice(start, start + size), slice(left, left + 128))
                base_ref[piece] = x_scr[piece].astype(F32) + column * total[piece]


def sixth_kernel(others, mp, tiles, *refs):
    qa_refs, qb_refs, state_refs = (refs[i * others : (i + 1) * others] for i in range(3))
    w0_ref, w1_ref, base_ref, gate_ref, out_ref, attn_scr, out_scr, sems = refs[3 * others :]
    m, mine = lax.axis_index("mp"), lax.axis_index("rep")
    cols, rows = out_ref.shape
    per_tile = rows // tiles
    width = attn_scr.shape[0]
    subs = w0_ref.shape[1] // width
    for index in range(others):
        attend((qa_refs[index], qb_refs[index]), state_refs[index], attn_scr, tiles)
        p = lax.rem(m + mp - 1 - index, mp)
        last = index == others - 1
        for source, ref in enumerate((w0_ref, w1_ref)):
            for s in range(subs):
                here = jnp.logical_and((p // subs == mine) == (source == 0), p % subs == s)

                @pl.when(here)
                def _(ref=ref, s=s, last=last):
                    for number, (start, size) in enumerate(pieces(cols)):
                        span = slice(start, start + size)
                        part = jnp.dot(
                            ref[span, s * width : (s + 1) * width], attn_scr[...],
                            preferred_element_type=F32,
                        )
                        for t in range(tiles):
                            column = gate_ref[span, t * 128 : (t + 1) * 128]
                            for left in range(t * per_tile, (t + 1) * per_tile, 128):
                                lanes = slice(left, left + 128)
                                value = base_ref[span, lanes] + column * part[:, lanes]
                                if last:
                                    out_scr[span, lanes] = value.astype(BF16)
                                else:
                                    base_ref[span, lanes] = value
                        if last:
                            pltpu.make_async_copy(
                                out_scr.at[span], out_ref.at[span], sems.at[number]
                            ).start()
    for number, (start, size) in enumerate(pieces(cols)):
        span = slice(start, start + size)
        pltpu.make_async_copy(out_scr.at[span], out_ref.at[span], sems.at[number]).wait()


def pieces(cols):
    unit = cols // 16 // 4 * 16
    return [(0, cols - 2 * unit), (cols - 2 * unit, unit), (cols - unit, unit)]


def seq_order(seq):
    return [*range((seq + 1) // 2, seq), *range(1, (seq + 1) // 2)]


def body(tokens, slot_image, modulation, w_qkv, w_out, *, seq, mp):
    rows, depth = tokens.shape
    tiles = slot_image.shape[0]
    half, _, width = w_qkv.shape
    heads_half, cols = w_out.shape
    swap = [(0, 1), (1, 0)]
    in_hbm = functools.partial(pltpu.with_memory_space_constraint, memory_space=pltpu.HBM)
    shape = jax.ShapeDtypeStruct
    x = in_hbm(tokens.T)
    w = in_hbm(jnp.transpose(w_qkv, (1, 0, 2)))
    wo = w_out.T
    dma = pltpu.SemaphoreType.DMA

    def shift(value, axis, size, by):
        return lax.ppermute(value, axis, [(i, (i + by) % size) for i in range(size)])

    def swap_seq(value, d):
        if seq & (seq - 1):
            return shift(value, "seq", seq, d)
        return lax.ppermute(value, "seq", [(i, i ^ d) for i in range(seq)])

    def across(value):
        return lax.ppermute(value, "rep", swap)

    lead = min(384, -(-width // 256) * 128)
    cuts = [(0, lead), (lead, width - lead)]
    kv_shapes, kv_spans = [], []
    for out, (start, size) in enumerate(cuts):
        joined = size % 128 == 0
        kv_shapes.append((1, half, 2 * size) if joined else (2, half, size))
        for c in range(2):
            kv_spans.append((out, 1 + c, start, size, 0 if joined else c, c * size if joined else 0))
    part_shapes = [shape((a, rows, c), F32) for a, _, c in kv_shapes]

    def norm(begin, end, inputs, spans, loaded, before=(), known=()):
        spaces = [HB, VM, VM, HB] if begin else [HB] * 4
        scratch = [
            pltpu.SMEM((tiles,), jnp.int32), pltpu.VMEM((tiles, 8, half), F32),
            dma((3 + (end - begin) // 128 + len(spans),)),
        ]
        if not begin:
            scratch += [pltpu.VMEM((depth, end), BF16), pltpu.VMEM(modulation.shape, F32)]
        return call(
            functools.partial(norm_kernel, begin, end, spans, len(loaded)),
            [shape((rows, half), BF16)] * 2 + [shape(l, BF16) for l in loaded]
            + (part_shapes if known else []),
            spaces + [VM] * (len(before) + len(known)), scratch=scratch,
            aliases={4 + i: i for i in range(len(before))}, nbytes=4 * MIB,
        )(*inputs, w, *before, *known)

    split = rows // 256 * 128
    own, other, wa, *kv, x_last = norm(
        0, split, (in_hbm(slot_image), x, in_hbm(modulation)),
        [(0, 0, 0, lead, 0, 0)] + [(1 + out, *rest) for out, *rest in kv_spans],
        [(1, half, lead)] + kv_shapes + [(depth, rows - split)],
    )
    wa_theirs = across(wa)
    kv_theirs = [across(k) for k in kv]
    own, other, wb, *part = norm(
        split, rows, (slot_image, x_last, modulation), [(0, 0, lead, width - lead, 0, 0)],
        [(1, half, width - lead)], (own, other), kv,
    )
    wb_theirs = across(wb)

    def query(size, mine, theirs):
        return call(
            query_kernel, shape((rows, size), BF16), [VM] * 4,
            flops=2 * rows * depth * size, nbytes=3 * MIB,
        )(own, other, mine, theirs)

    qa = query(lead, wa[0], wa_theirs[0])
    qa_theirs = [shift(qa, "mp", mp, d) for d in range(1, mp)]
    part = call(
        functools.partial(part_kernel, split), part_shapes, [VM] * 6,
        aliases={4: 0, 5: 1}, flops=2 * rows * half * width, nbytes=4 * MIB,
    )(own, *kv, qa, *part)
    block = (state_rows(tiles), width)
    state = ()
    for i, (start, size) in enumerate(cuts):
        state = (call(
            functools.partial(second_kernel, start), shape(block, BF16),
            [HB] + [VM] * (3 + len(state)), aliases={4: 0} if state else None,
            scratch=[pltpu.VMEM((rows, size), BF16)] * 2 + [pltpu.SMEM((tiles,), jnp.int32), dma],
            flops=2 * rows * half * 2 * size, nbytes=6 * MIB,
        )(slot_image, other, kv_theirs[i], part[i], *state),)
    state = state[0]
    near = [state] + [swap_seq(state, d) for d in seq_order(seq)]
    qb = query(width - lead, wb[0], wb_theirs[0])
    qb_theirs = [shift(qb, "mp", mp, d) for d in range(1, mp)]
    wo_theirs = across(wo)
    far = [across(b) for b in near]
    so_far = call(sum_kernel, shape(block, F32), [VM] * (2 * seq - 1), nbytes=MIB)(*near, *far[:-1])
    wide, final = call(
        last_kernel, [shape(block, F32), shape(block, BF16)], [VM] * 3, nbytes=MIB
    )(near[0], so_far, far[-1])
    finals = [shift(final, "mp", mp, d) for d in range(1, mp)]
    base, gate = call(
        fifth_kernel, [shape((cols, rows), F32), shape((cols, tiles * 128), F32)],
        [HB, VM, VM, VM, HB, HB, HB, HB],
        scratch=[
            pltpu.VMEM((width, rows), BF16), pltpu.VMEM((cols, heads_half), BF16), pltpu.VMEM((cols, rows), BF16),
            pltpu.VMEM(modulation.shape, F32), pltpu.SMEM((tiles,), jnp.int32), dma((4,)),
        ],
        flops=2 * rows * width * cols, nbytes=4 * MIB,
    )(slot_image, qa, qb, wide, wo, wo_theirs, x, modulation)
    out = call(
        functools.partial(sixth_kernel, mp - 1, mp, tiles), shape((cols, rows), BF16),
        [VM] * (3 * (mp - 1) + 4), out_specs=HB,
        scratch=[pltpu.VMEM((width, rows), BF16), pltpu.VMEM((cols, rows), BF16), dma((3,))],
        flops=2 * rows * width * cols, nbytes=4 * MIB,
    )(*qa_theirs, *qb_theirs, *finals, wo, wo_theirs, base, gate)
    return out.T


def solution(mesh):
    sizes = dict(mesh.shape)

    def step(*args):
        return body(*args, seq=sizes["seq"], mp=sizes["mp"])

    return jax.shard_map(
        step,
        mesh=mesh,
        in_specs=(
            P(("groups", "seq", "rep"), None),
            P(("groups", "seq", "rep")),
            P("groups", None, None),
            P("rep", None, "mp"),
            P("rep", "mp"),
        ),
        out_specs=P(("groups", "seq", "rep"), "mp"),
        check_vma=False,
    )
```

```python
import functools

import jax
import jax.numpy as jnp
from jax import lax
from jax.experimental import pallas as pl
from jax.experimental.pallas import tpu as pltpu
from jax.sharding import PartitionSpec as P

HD = 32
F32 = jnp.float32
BF16 = jnp.bfloat16
VM = pl.BlockSpec(memory_space=pltpu.VMEM)
HB = pl.BlockSpec(memory_space=pltpu.HBM)
MIB = 1 << 20


def call(kernel, out_shape, in_specs, out_specs=None, scratch=(), vmem=16, aliases=None, flops=0, nbytes=0):
    if out_specs is None:
        out_specs = [VM] * len(out_shape) if isinstance(out_shape, list) else VM
    return pl.pallas_call(
        kernel,
        out_shape=out_shape,
        in_specs=in_specs,
        out_specs=out_specs,
        scratch_shapes=list(scratch),
        input_output_aliases=aliases or {},
        compiler_params=pltpu.CompilerParams(vmem_limit_bytes=vmem * MIB),
        cost_estimate=pl.CostEstimate(flops=flops, bytes_accessed=nbytes, transcendentals=0),
    )


def column_sum(ref, at, function):
    rows = ref.shape[0]
    total = jnp.zeros((8, 128), F32)
    for start in range(0, rows, 64):
        size = min(64, rows - start)
        value = function(ref[start : start + size, at].astype(F32))
        total += jnp.sum(value.reshape(size // 8, 8, value.shape[1]), axis=0)
    return jnp.sum(total, axis=0, keepdims=True)


def norm_kernel(begin, end, spans, loaded, img_ref, x_ref, mods_ref, w_ref, *refs):
    known = refs[2:3] if begin else ()
    refs = refs[len(known) + 2 :] if begin else refs
    own_ref, other_ref = refs[:2]
    load_refs, refs = refs[2 : 2 + loaded], refs[2 + loaded :]
    part_refs = refs[: 2 * len(known)]
    img_scr, sel_scr, sems, *more = refs[2 * len(known) :]
    mine = lax.axis_index("rep")
    rows, half = own_ref.shape
    width_in = x_ref.shape[0]
    tiles = img_ref.shape[0]
    step = 128
    per_tile = rows // tiles
    steps = (end - begin) // step
    early = [pltpu.make_async_copy(img_ref, img_scr, sems.at[0])]
    x_copies = [None] * steps
    copies = []
    if not begin:
        x_scr, mods_scr = more
        early.append(pltpu.make_async_copy(mods_ref, mods_scr, sems.at[1]))
        x_copies = [
            pltpu.make_async_copy(
                x_ref.at[:, pl.ds(i * step, step)], x_scr.at[:, pl.ds(i * step, step)], sems.at[3 + i]
            )
            for i in range(steps)
        ]
        copies.append(pltpu.make_async_copy(x_ref.at[:, pl.ds(end, rows - end)], load_refs[-1], sems.at[2]))
        for copy in x_copies[:1] + early + x_copies[1:]:
            copy.start()
        x_ref, mods_ref = x_scr, mods_scr
    else:
        early[0].start()
    copies = [
        pltpu.make_async_copy(
            w_ref.at[plane, :, pl.ds(start, size)], load_refs[out].at[at, :, pl.ds(left, size)],
            sems.at[3 + steps + i],
        )
        for i, (out, plane, start, size, at, left) in enumerate(spans)
    ] + copies
    for copy in copies:
        copy.start()
    known_late = (load_refs[0],) if begin else ()
    products = product_list(own_ref, known, part_refs[:1], slice(0, begin))
    if begin:
        late = product_list(own_ref, known_late, part_refs[1:], slice(0, begin))
        pending = copies[: len(spans) - 1]
        products += [functools.partial(run_after, pending, late[0])] + late[1:]
        copies = copies[len(pending) :]
    total = steps * 2 * -(-half // step)
    count, done = 0, 0
    for index in range(steps):
        start = begin + index * step
        at = slice(start, start + step)
        t = start // per_tile
        x_at = slice(index * step, (index + 1) * step)
        if x_copies[index] is not None:
            x_copies[index].wait()
        mean = column_sum(x_ref, x_at, lambda v: v) / width_in
        var = column_sum(x_ref, x_at, lambda v: (v - mean) ** 2) / width_in
        inv = 1.0 / jnp.sqrt(var + 1e-06)
        mean = jnp.broadcast_to(mean, (step, step)).T
        inv = jnp.broadcast_to(inv, (step, step)).T
        if not index:
            for copy in early:
                copy.wait()
        if not index or start % per_tile == 0:
            mods = mods_ref[img_scr[t]]
            for row in range(2):
                low, high = mods[row : row + 1, :half], mods[row : row + 1, half:]
                if row:
                    low, high = 1.0 + low, 1.0 + high
                sel_scr[t, row : row + 1] = jnp.where(mine == 0, low, high)
                sel_scr[t, 2 + row : 3 + row] = jnp.where(mine == 0, high, low)
        for which, out in enumerate((own_ref, other_ref)):
            base = (mine if which == 0 else 1 - mine) * half
            for left in range(0, half, step):
                size = min(step, half - left)
                first = pl.multiple_of(base + left, 16)
                value = x_ref[pl.ds(first, size), x_at].T.astype(F32)
                lanes = slice(left, left + size)
                shift = sel_scr[t, 2 * which : 2 * which + 1, lanes]
                scale = sel_scr[t, 2 * which + 1 : 2 * which + 2, lanes]
                out[at, lanes] = (
                    (value - mean[:, :size]) * inv[:, :size] * scale + shift
                ).astype(BF16)
                count += 1
                while done * total < count * len(products):
                    products[done]()
                    done += 1
    for copy in copies:
        copy.wait()


def run_after(copies, function):
    for copy in copies:
        copy.wait()
    function()


def product_list(own_ref, w_refs, part_refs, rows):
    def product(w_ref, part_ref, c, lanes):
        part_ref[c, rows, lanes] = jnp.dot(
            own_ref[rows, :], w_ref[c, :, lanes], preferred_element_type=F32
        )

    return [
        functools.partial(product, w_ref, part_ref, c, slice(at, min(at + 256, w_ref.shape[2])))
        for w_ref, part_ref in zip(w_refs, part_refs)
        for c in range(w_ref.shape[0])
        for at in range(0, w_ref.shape[2], 256)
    ]


def query_kernel(own_ref, other_ref, w_ref, w_other_ref, q_ref):
    total = jnp.dot(own_ref[...], w_ref[...], preferred_element_type=F32)
    total += jnp.dot(other_ref[...], w_other_ref[...], preferred_element_type=F32)
    q_ref[...] = jnp.maximum(total, 0.0).astype(BF16)


def part_kernel(begin, own_ref, w0_ref, w1_ref, after_ref, *refs):
    outs = refs[-2:]
    for product in product_list(own_ref, (w0_ref, w1_ref), outs, slice(begin, own_ref.shape[0])):
        product()


def head_blocks(width):
    return [(start, min(128, width - start)) for start in range(0, width, 128)]


def same_head(rows, cols):
    return (
        lax.broadcasted_iota(jnp.int32, (rows, cols), 0) // HD
        == lax.broadcasted_iota(jnp.int32, (rows, cols), 1) // HD
    )


def state_rows(tiles):
    return tiles * HD + 8


def second_kernel(offset, img_ref, mod_ref, w_ref, part_ref, *refs):
    state_ref, k_scr, v_scr, img_scr, sem = refs[-5:]
    rows, width = k_scr.shape
    tiles = img_ref.shape[0]
    per_tile = rows // tiles
    img_copy = pltpu.make_async_copy(img_ref, img_scr, sem)
    img_copy.start()
    mod = mod_ref[...]
    for c in range(w_ref.shape[0]):
        total = part_ref[c] + jnp.dot(mod, w_ref[c], preferred_element_type=F32)
        if c == 0:
            k_scr[...] = jnp.maximum(total[:, :width], 0.0).astype(BF16)
        if c == w_ref.shape[0] - 1:
            v_scr[...] = total[:, total.shape[1] - width :].astype(BF16)
    img_copy.wait()
    sums, images = [], []
    for t in range(tiles):
        span = slice(t * per_tile, (t + 1) * per_tile)
        sums.append(jnp.sum(k_scr[span, :].astype(F32), axis=0, keepdims=True))
        images.append(jnp.full((1, width), img_scr[t].astype(F32), F32))
        for start, size in head_blocks(width):
            full = lax.dot_general(
                v_scr[span, start : start + size],
                k_scr[span, start : start + size],
                (((0,), (0,)), ((), ())),
                preferred_element_type=F32,
            )
            full = jnp.where(same_head(size, size), full, 0.0)
            state_ref[t * HD : (t + 1) * HD, offset + start : offset + start + size] = sum(
                full[j * HD : (j + 1) * HD, :] for j in range(size // HD)
            ).astype(BF16)
    state_ref[tiles * HD :, offset : offset + width] = tail_rows(sums, images).astype(BF16)


def tail_rows(sums, images):
    rest = [s - s.astype(BF16).astype(F32) for s in sums]
    rows = sums + rest + images
    rows.append(jnp.zeros((8 - len(rows), sums[0].shape[1]), F32))
    return jnp.concatenate(rows, axis=0)


def add_states(totals, sums, want, blocks, tiles):
    for ref in blocks:
        tail = ref[tiles * HD :, :].astype(F32)
        for s in range(tiles):
            state = ref[s * HD : (s + 1) * HD, :].astype(F32)
            ksum = tail[s : s + 1] + tail[tiles + s : tiles + s + 1]
            for t in range(tiles):
                keep = (tail[2 * tiles + s : 2 * tiles + s + 1] == want[t : t + 1]).astype(F32)
                totals[t] += keep * state
                sums[t] += keep * ksum


def wanted(ref, tiles):
    return ref[tiles * HD :, :].astype(F32)[2 * tiles : 3 * tiles]


def sum_kernel(known, *refs):
    own_ref, their_ref, before, blocks = refs[0], refs[1], refs[2 : 2 + known], refs[2 + known : -2]
    outs = refs[-2:]
    width = own_ref.shape[1]
    tiles = (own_ref.shape[0] - 8) // HD
    for side, (ref, out) in enumerate(zip((own_ref, their_ref), outs)):
        if known:
            totals = [before[side][t * HD : (t + 1) * HD, :] for t in range(tiles)]
            tail = before[side][tiles * HD :, :]
            sums = [tail[t : t + 1] for t in range(tiles)]
        else:
            totals = [jnp.zeros((HD, width), F32)] * tiles
            sums = [jnp.zeros((1, width), F32)] * tiles
        add_states(totals, sums, wanted(ref, tiles), blocks, tiles)
        for t in range(tiles):
            out[t * HD : (t + 1) * HD, :] = totals[t]
        out[tiles * HD :, :] = jnp.concatenate(
            sums + [jnp.zeros((8 - tiles, width), F32)], axis=0
        )


def last_kernel(mine_ref, theirs_ref, wide_ref, out_ref):
    tiles = (out_ref.shape[0] - 8) // HD
    states = slice(0, tiles * HD)
    total = mine_ref[states, :] + theirs_ref[states, :]
    wide_ref[states, :] = total
    out_ref[states, :] = total.astype(BF16)
    tail = mine_ref[tiles * HD :, :] + theirs_ref[tiles * HD :, :]
    tail = tail_rows([tail[t : t + 1] for t in range(tiles)], [])
    wide_ref[tiles * HD :, :] = tail
    out_ref[tiles * HD :, :] = tail.astype(BF16)


def attend(q_refs, state_ref, out_ref, tiles):
    width, rows = out_ref.shape
    per_tile = rows // tiles
    first = q_refs[0].shape[1]
    exact = state_ref.dtype == F32
    tail = state_ref[tiles * HD :, :].astype(F32)
    for t in range(tiles):
        span = slice(t * per_tile, (t + 1) * per_tile)
        for start, size in head_blocks(width):
            lanes = slice(start, start + size)
            mask = same_head(size, size)
            state = state_ref[t * HD : (t + 1) * HD, lanes].astype(F32)
            state = jnp.concatenate([state] * (size // HD), axis=0)
            heads = size // HD
            parts = [jnp.where(mask, state, 0.0)]
            if exact:
                parts.append(parts[0] - parts[0].astype(BF16).astype(F32))
            row = lax.broadcasted_iota(jnp.int32, (8, size), 0)
            head = lax.broadcasted_iota(jnp.int32, (8, size), 1) // HD
            sums = jnp.where(row < 4, tail[t : t + 1, lanes], tail[tiles + t : tiles + t + 1, lanes])
            parts.append(jnp.where(row % 4 == head, sums, 0.0))
            left = jnp.concatenate(parts, axis=0).astype(BF16)
            both = lax.dot_general(
                left,
                q_refs[0][span, lanes] if start < first else q_refs[1][span, start - first : start - first + size],
                (((1,), (1,)), ((), ())), preferred_element_type=F32,
            )
            numer = both[:size]
            if exact:
                numer += both[size : 2 * size]
            sums = both[-8:]
            inverse = 1.0 / (sums[:4] + sums[4:] + 1e-06)
            inverse = jnp.concatenate(
                [jnp.broadcast_to(inverse[j : j + 1], (HD, per_tile)) for j in range(heads)], axis=0
            )
            out_ref[start : start + size, span] = (numer * inverse).astype(BF16)


def fetch_weights(p, width, w_refs, w_scr, sem):
    mine = lax.axis_index("rep")
    subs = w_refs[0].shape[1] // width
    for source, ref in enumerate(w_refs):
        @pl.when((p // subs == mine) == (source == 0))
        def _():
            pltpu.make_async_copy(ref, w_scr, sem).start()

    def finish():
        pltpu.make_async_copy(w_refs[0], w_scr, sem).wait()
        weights = w_scr[...]
        chosen = weights[:, :width]
        for s in range(1, subs):
            chosen = jnp.where(p % subs == s, weights[:, s * width : (s + 1) * width], chosen)
        return chosen

    return finish


def fifth_kernel(
    img_ref, qa_ref, qb_ref, state_ref, w0_ref, w1_ref, x_ref, mods_ref, base_ref, gate_ref,
    attn_scr, w_scr, x_scr, gates_scr, img_scr, sems,
):
    m = lax.axis_index("mp")
    cols, rows = base_ref.shape
    tiles = img_ref.shape[0]
    per_tile = rows // tiles
    finish = fetch_weights(m, attn_scr.shape[0], (w0_ref, w1_ref), w_scr, sems.at[0])
    copies = [
        pltpu.make_async_copy(img_ref, img_scr, sems.at[1]),
        pltpu.make_async_copy(x_ref.at[pl.ds(m * cols, cols), :], x_scr, sems.at[2]),
        pltpu.make_async_copy(mods_ref, gates_scr, sems.at[3]),
    ]
    for copy in copies:
        copy.start()
    attend((qa_ref, qb_ref), state_ref, attn_scr, tiles)
    weights = finish()
    for copy in copies:
        copy.wait()
    total = jnp.dot(weights, attn_scr[...], preferred_element_type=F32)
    for t in range(tiles):
        gates = gates_scr[img_scr[t]][2:3]
        gate = gates[:, :cols]
        for p in range(1, gates.shape[1] // cols):
            gate = jnp.where(m == p, gates[:, p * cols : (p + 1) * cols], gate)
        for start in range(0, cols, 128):
            size = min(128, cols - start)
            column = jnp.broadcast_to(gate[:, start : start + size], (128, size)).T
            gate_ref[start : start + size, t * 128 : (t + 1) * 128] = column
            for left in range(t * per_tile, (t + 1) * per_tile, 128):
                piece = (slice(start, start + size), slice(left, left + 128))
                base_ref[piece] = x_scr[piece].astype(F32) + column * total[piece]


def sixth_kernel(others, mp, tiles, *refs):
    qa_refs, qb_refs, state_refs = (refs[i * others : (i + 1) * others] for i in range(3))
    w0_ref, w1_ref, base_ref, gate_ref, out_ref, attn_scr, out_scr, sems = refs[3 * others :]
    m, mine = lax.axis_index("mp"), lax.axis_index("rep")
    cols, rows = out_ref.shape
    per_tile = rows // tiles
    width = attn_scr.shape[0]
    subs = w0_ref.shape[1] // width
    for index in range(others):
        attend((qa_refs[index], qb_refs[index]), state_refs[index], attn_scr, tiles)
        p = lax.rem(m + mp - 1 - index, mp)
        last = index == others - 1
        for source, ref in enumerate((w0_ref, w1_ref)):
            for s in range(subs):
                here = jnp.logical_and((p // subs == mine) == (source == 0), p % subs == s)

                @pl.when(here)
                def _(ref=ref, s=s, last=last):
                    for number, (start, size) in enumerate(pieces(cols)):
                        span = slice(start, start + size)
                        part = jnp.dot(
                            ref[span, s * width : (s + 1) * width], attn_scr[...],
                            preferred_element_type=F32,
                        )
                        for t in range(tiles):
                            column = gate_ref[span, t * 128 : (t + 1) * 128]
                            for left in range(t * per_tile, (t + 1) * per_tile, 128):
                                lanes = slice(left, left + 128)
                                value = base_ref[span, lanes] + column * part[:, lanes]
                                if last:
                                    out_scr[span, lanes] = value.astype(BF16)
                                else:
                                    base_ref[span, lanes] = value
                        if last:
                            pltpu.make_async_copy(
                                out_scr.at[span], out_ref.at[span], sems.at[number]
                            ).start()
    for number, (start, size) in enumerate(pieces(cols)):
        span = slice(start, start + size)
        pltpu.make_async_copy(out_scr.at[span], out_ref.at[span], sems.at[number]).wait()


def pieces(cols):
    unit = cols // 16 // 4 * 16
    return [(0, cols - 2 * unit), (cols - 2 * unit, unit), (cols - unit, unit)]


def seq_order(seq):
    return [*range((seq + 1) // 2, seq), *range(1, (seq + 1) // 2)]


def body(tokens, slot_image, modulation, w_qkv, w_out, *, seq, mp):
    rows, depth = tokens.shape
    tiles = slot_image.shape[0]
    half, _, width = w_qkv.shape
    heads_half, cols = w_out.shape
    swap = [(0, 1), (1, 0)]
    in_hbm = functools.partial(pltpu.with_memory_space_constraint, memory_space=pltpu.HBM)
    shape = jax.ShapeDtypeStruct
    x = in_hbm(tokens.T)
    w = in_hbm(jnp.transpose(w_qkv, (1, 0, 2)))
    wo = w_out.T
    dma = pltpu.SemaphoreType.DMA

    def shift(value, axis, size, by):
        return lax.ppermute(value, axis, [(i, (i + by) % size) for i in range(size)])

    def swap_seq(value, d):
        if seq & (seq - 1):
            return shift(value, "seq", seq, d)
        return lax.ppermute(value, "seq", [(i, i ^ d) for i in range(seq)])

    def across(value):
        return lax.ppermute(value, "rep", swap)

    lead = min(384, -(-width // 256) * 128)
    cuts = [(0, lead), (lead, width - lead)]
    kv_shapes, kv_spans = [], []
    for out, (start, size) in enumerate(cuts):
        joined = size % 128 == 0
        kv_shapes.append((1, half, 2 * size) if joined else (2, half, size))
        for c in range(2):
            kv_spans.append((out, 1 + c, start, size, 0 if joined else c, c * size if joined else 0))
    part_shapes = [shape((a, rows, c), F32) for a, _, c in kv_shapes]

    def norm(begin, end, inputs, spans, loaded, before=(), known=()):
        spaces = [HB, VM, VM, HB] if begin else [HB] * 4
        scratch = [
            pltpu.SMEM((tiles,), jnp.int32), pltpu.VMEM((tiles, 8, half), F32),
            dma((3 + (end - begin) // 128 + len(spans),)),
        ]
        if not begin:
            scratch += [pltpu.VMEM((depth, end), BF16), pltpu.VMEM(modulation.shape, F32)]
        return call(
            functools.partial(norm_kernel, begin, end, spans, len(loaded)),
            [shape((rows, half), BF16)] * 2 + [shape(l, BF16) for l in loaded]
            + (part_shapes if known else []),
            spaces + [VM] * (len(before) + len(known)), scratch=scratch,
            aliases={4 + i: i for i in range(len(before))}, nbytes=4 * MIB,
        )(*inputs, w, *before, *known)

    split = rows // 256 * 128
    own, other, wa, kv_0, x_last = norm(
        0, split, (in_hbm(slot_image), x, in_hbm(modulation)),
        [(0, 0, 0, lead, 0, 0)] + [(1, *rest) for out, *rest in kv_spans if out == 0],
        [(1, half, lead), kv_shapes[0], (depth, rows - split)],
    )
    wa_theirs = across(wa)
    kv_theirs = [across(kv_0)]
    own, other, kv_1, wb, *part = norm(
        split, rows, (slot_image, x_last, modulation),
        [(0, *rest) for out, *rest in kv_spans if out == 1] + [(1, 0, lead, width - lead, 0, 0)],
        [kv_shapes[1], (1, half, width - lead)], (own, other), (kv_0,),
    )
    kv = [kv_0, kv_1]
    kv_theirs.append(across(kv_1))
    wb_theirs = across(wb)

    def query(size, mine, theirs):
        return call(
            query_kernel, shape((rows, size), BF16), [VM] * 4,
            flops=2 * rows * depth * size, nbytes=3 * MIB,
        )(own, other, mine, theirs)

    qa = query(lead, wa[0], wa_theirs[0])
    qa_theirs = [shift(qa, "mp", mp, d) for d in range(1, mp)]
    part = call(
        functools.partial(part_kernel, split), part_shapes, [VM] * 6,
        aliases={4: 0, 5: 1}, flops=2 * rows * half * width, nbytes=4 * MIB,
    )(own, *kv, qa, *part)
    block = (state_rows(tiles), width)
    state = ()
    for i, (start, size) in enumerate(cuts):
        state = (call(
            functools.partial(second_kernel, start), shape(block, BF16),
            [HB] + [VM] * (3 + len(state)), aliases={4: 0} if state else None,
            scratch=[pltpu.VMEM((rows, size), BF16)] * 2 + [pltpu.SMEM((tiles,), jnp.int32), dma],
            flops=2 * rows * half * 2 * size, nbytes=6 * MIB,
        )(slot_image, other, kv_theirs[i], part[i], *state),)
    state = state[0]
    near = [state] + [swap_seq(state, d) for d in seq_order(seq)]
    qb = query(width - lead, wb[0], wb_theirs[0])
    qb_theirs = [shift(qb, "mp", mp, d) for d in range(1, mp)]
    wo_theirs = across(wo)
    their_state = across(state)
    both = [shape(block, F32)] * 2
    begun = call(functools.partial(sum_kernel, 0), both, [VM] * 4, nbytes=MIB)(
        state, their_state, *near[:2]
    )
    mine, theirs = call(
        functools.partial(sum_kernel, 2), both, [VM] * (2 + seq), nbytes=MIB
    )(state, their_state, *begun, *near[2:])
    wide, final = call(
        last_kernel, [shape(block, F32), shape(block, BF16)], [VM] * 2, nbytes=MIB
    )(mine, across(theirs))
    finals = [shift(final, "mp", mp, d) for d in range(1, mp)]
    base, gate = call(
        fifth_kernel, [shape((cols, rows), F32), shape((cols, tiles * 128), F32)],
        [HB, VM, VM, VM, HB, HB, HB, HB],
        scratch=[
            pltpu.VMEM((width, rows), BF16), pltpu.VMEM((cols, heads_half), BF16), pltpu.VMEM((cols, rows), BF16),
            pltpu.VMEM(modulation.shape, F32), pltpu.SMEM((tiles,), jnp.int32), dma((4,)),
        ],
        flops=2 * rows * width * cols, nbytes=4 * MIB,
    )(slot_image, qa, qb, wide, wo, wo_theirs, x, modulation)
    out = call(
        functools.partial(sixth_kernel, mp - 1, mp, tiles), shape((cols, rows), BF16),
        [VM] * (3 * (mp - 1) + 4), out_specs=HB,
        scratch=[pltpu.VMEM((width, rows), BF16), pltpu.VMEM((cols, rows), BF16), dma((3,))],
        flops=2 * rows * width * cols, nbytes=4 * MIB,
    )(*qa_theirs, *qb_theirs, *finals, wo, wo_theirs, base, gate)
    return out.T


def solution(mesh):
    sizes = dict(mesh.shape)

    def step(*args):
        return body(*args, seq=sizes["seq"], mp=sizes["mp"])

    return jax.shard_map(
        step,
        mesh=mesh,
        in_specs=(
            P(("groups", "seq", "rep"), None),
            P(("groups", "seq", "rep")),
            P("groups", None, None),
            P("rep", None, "mp"),
            P("rep", "mp"),
        ),
        out_specs=P(("groups", "seq", "rep"), "mp"),
        check_vma=False,
    )
```

```python
import functools

import jax
import jax.numpy as jnp
from jax import lax
from jax.experimental import pallas as pl
from jax.experimental.pallas import tpu as pltpu
from jax.sharding import PartitionSpec as P

HD = 32
F32 = jnp.float32
BF16 = jnp.bfloat16
VM = pl.BlockSpec(memory_space=pltpu.VMEM)
HB = pl.BlockSpec(memory_space=pltpu.HBM)
MIB = 1 << 20


def call(kernel, out_shape, in_specs, out_specs=None, scratch=(), vmem=16, aliases=None, flops=0, nbytes=0):
    if out_specs is None:
        out_specs = [VM] * len(out_shape) if isinstance(out_shape, list) else VM
    return pl.pallas_call(
        kernel,
        out_shape=out_shape,
        in_specs=in_specs,
        out_specs=out_specs,
        scratch_shapes=list(scratch),
        input_output_aliases=aliases or {},
        compiler_params=pltpu.CompilerParams(vmem_limit_bytes=vmem * MIB),
        cost_estimate=pl.CostEstimate(flops=flops, bytes_accessed=nbytes, transcendentals=0),
    )


def column_sum(ref, at, function):
    rows = ref.shape[0]
    total = jnp.zeros((8, 128), F32)
    for start in range(0, rows, 64):
        size = min(64, rows - start)
        value = function(ref[start : start + size, at].astype(F32))
        total += jnp.sum(value.reshape(size // 8, 8, value.shape[1]), axis=0)
    return jnp.sum(total, axis=0, keepdims=True)


def norm_kernel(begin, end, spans, loaded, img_ref, x_ref, mods_ref, w_ref, *refs):
    known = refs[2:5] if begin else ()
    refs = refs[len(known) + 2 :] if begin else refs
    own_ref, other_ref = refs[:2]
    load_refs, refs = refs[2 : 2 + loaded], refs[2 + loaded :]
    part_refs = refs[: len(known)]
    img_scr, sel_scr, sems, *more = refs[len(known) :]
    mine = lax.axis_index("rep")
    rows, half = own_ref.shape
    width_in = x_ref.shape[0]
    tiles = img_ref.shape[0]
    step = 128
    per_tile = rows // tiles
    steps = (end - begin) // step
    early = [pltpu.make_async_copy(img_ref, img_scr, sems.at[0])]
    x_copies = [None] * steps
    copies = []
    if not begin:
        x_scr, mods_scr = more
        early.append(pltpu.make_async_copy(mods_ref, mods_scr, sems.at[1]))
        x_copies = [
            pltpu.make_async_copy(
                x_ref.at[:, pl.ds(i * step, step)], x_scr.at[:, pl.ds(i * step, step)], sems.at[3 + i]
            )
            for i in range(steps)
        ]
        copies.append(pltpu.make_async_copy(x_ref.at[:, pl.ds(end, rows - end)], load_refs[-1], sems.at[2]))
        for copy in x_copies[:1] + early + x_copies[1:]:
            copy.start()
        x_ref, mods_ref = x_scr, mods_scr
    else:
        early[0].start()
    copies = [
        pltpu.make_async_copy(
            w_ref.at[plane, :, pl.ds(start, size)], load_refs[out].at[at, :, pl.ds(left, size)],
            sems.at[3 + steps + i],
        )
        for i, (out, plane, start, size, at, left) in enumerate(spans)
    ] + copies
    for copy in copies:
        copy.start()
    products = product_list(own_ref, known, part_refs, slice(0, begin))
    total = steps * 2 * -(-half // step)
    count, done = 0, 0
    for index in range(steps):
        start = begin + index * step
        at = slice(start, start + step)
        t = start // per_tile
        x_at = slice(index * step, (index + 1) * step)
        if x_copies[index] is not None:
            x_copies[index].wait()
        mean = column_sum(x_ref, x_at, lambda v: v) / width_in
        var = column_sum(x_ref, x_at, lambda v: (v - mean) ** 2) / width_in
        inv = 1.0 / jnp.sqrt(var + 1e-06)
        mean = jnp.broadcast_to(mean, (step, step)).T
        inv = jnp.broadcast_to(inv, (step, step)).T
        if not index:
            for copy in early:
                copy.wait()
        if not index or start % per_tile == 0:
            mods = mods_ref[img_scr[t]]
            for row in range(2):
                low, high = mods[row : row + 1, :half], mods[row : row + 1, half:]
                if row:
                    low, high = 1.0 + low, 1.0 + high
                sel_scr[t, row : row + 1] = jnp.where(mine == 0, low, high)
                sel_scr[t, 2 + row : 3 + row] = jnp.where(mine == 0, high, low)
        for which, out in enumerate((own_ref, other_ref)):
            base = (mine if which == 0 else 1 - mine) * half
            for left in range(0, half, step):
                size = min(step, half - left)
                first = pl.multiple_of(base + left, 16)
                value = x_ref[pl.ds(first, size), x_at].T.astype(F32)
                lanes = slice(left, left + size)
                shift = sel_scr[t, 2 * which : 2 * which + 1, lanes]
                scale = sel_scr[t, 2 * which + 1 : 2 * which + 2, lanes]
                out[at, lanes] = (
                    (value - mean[:, :size]) * inv[:, :size] * scale + shift
                ).astype(BF16)
                count += 1
                while done * total < count * len(products):
                    products[done]()
                    done += 1
    for copy in copies:
        copy.wait()


def product_list(own_ref, w_refs, part_refs, rows):
    def product(w_ref, part_ref, c, lanes):
        part_ref[c, rows, lanes] = jnp.dot(
            own_ref[rows, :], w_ref[c, :, lanes], preferred_element_type=F32
        )

    return [
        functools.partial(product, w_ref, part_ref, c, slice(at, min(at + 256, w_ref.shape[2])))
        for w_ref, part_ref in zip(w_refs, part_refs)
        for c in range(w_ref.shape[0])
        for at in range(0, w_ref.shape[2], 256)
    ]


def query_kernel(begin, own_ref, other_ref, w_ref, w_other_ref, *refs):
    q_ref = refs[-1]
    for first, end in ((0, begin), (begin, own_ref.shape[0])):
        if first == end:
            continue
        total = jnp.dot(other_ref[first:end, :], w_other_ref[...], preferred_element_type=F32)
        if first < begin:
            total += refs[0][0, first:end, :]
        else:
            total += jnp.dot(own_ref[first:end, :], w_ref[...], preferred_element_type=F32)
        q_ref[first:end, :] = jnp.maximum(total, 0.0).astype(BF16)


def part_kernel(begin, own_ref, w0_ref, w1_ref, after_ref, *refs):
    outs = refs[-2:]
    for product in product_list(own_ref, (w0_ref, w1_ref), outs, slice(begin, own_ref.shape[0])):
        product()


def head_blocks(width):
    return [(start, min(128, width - start)) for start in range(0, width, 128)]


def same_head(rows, cols):
    return (
        lax.broadcasted_iota(jnp.int32, (rows, cols), 0) // HD
        == lax.broadcasted_iota(jnp.int32, (rows, cols), 1) // HD
    )


def state_rows(tiles):
    return tiles * HD + 8


def second_kernel(offset, img_ref, mod_ref, w_ref, part_ref, *refs):
    state_ref, k_scr, v_scr, img_scr, sem = refs[-5:]
    rows, width = k_scr.shape
    tiles = img_ref.shape[0]
    per_tile = rows // tiles
    img_copy = pltpu.make_async_copy(img_ref, img_scr, sem)
    img_copy.start()
    mod = mod_ref[...]
    for c in range(w_ref.shape[0]):
        total = part_ref[c] + jnp.dot(mod, w_ref[c], preferred_element_type=F32)
        if c == 0:
            k_scr[...] = jnp.maximum(total[:, :width], 0.0).astype(BF16)
        if c == w_ref.shape[0] - 1:
            v_scr[...] = total[:, total.shape[1] - width :].astype(BF16)
    img_copy.wait()
    sums, images = [], []
    for t in range(tiles):
        span = slice(t * per_tile, (t + 1) * per_tile)
        sums.append(jnp.sum(k_scr[span, :].astype(F32), axis=0, keepdims=True))
        images.append(jnp.full((1, width), img_scr[t].astype(F32), F32))
        for start, size in head_blocks(width):
            full = lax.dot_general(
                v_scr[span, start : start + size],
                k_scr[span, start : start + size],
                (((0,), (0,)), ((), ())),
                preferred_element_type=F32,
            )
            full = jnp.where(same_head(size, size), full, 0.0)
            state_ref[t * HD : (t + 1) * HD, offset + start : offset + start + size] = sum(
                full[j * HD : (j + 1) * HD, :] for j in range(size // HD)
            ).astype(BF16)
    state_ref[tiles * HD :, offset : offset + width] = tail_rows(sums, images).astype(BF16)


def tail_rows(sums, images):
    rest = [s - s.astype(BF16).astype(F32) for s in sums]
    rows = sums + rest + images
    rows.append(jnp.zeros((8 - len(rows), sums[0].shape[1]), F32))
    return jnp.concatenate(rows, axis=0)


def add_states(totals, sums, want, blocks, tiles):
    for ref in blocks:
        tail = ref[tiles * HD :, :].astype(F32)
        for s in range(tiles):
            state = ref[s * HD : (s + 1) * HD, :].astype(F32)
            ksum = tail[s : s + 1] + tail[tiles + s : tiles + s + 1]
            for t in range(tiles):
                keep = (tail[2 * tiles + s : 2 * tiles + s + 1] == want[t : t + 1]).astype(F32)
                totals[t] += keep * state
                sums[t] += keep * ksum


def wanted(ref, tiles):
    return ref[tiles * HD :, :].astype(F32)[2 * tiles : 3 * tiles]


def sum_kernel(*refs):
    blocks, wide_ref = refs[:-1], refs[-1]
    width = wide_ref.shape[1]
    tiles = (wide_ref.shape[0] - 8) // HD
    totals = [jnp.zeros((HD, width), F32)] * tiles
    sums = [jnp.zeros((1, width), F32)] * tiles
    add_states(totals, sums, wanted(blocks[0], tiles), blocks, tiles)
    for t in range(tiles):
        wide_ref[t * HD : (t + 1) * HD, :] = totals[t]
    wide_ref[tiles * HD :, :] = jnp.concatenate(
        sums + [jnp.zeros((8 - tiles, width), F32)], axis=0
    )


def last_kernel(own_ref, so_far_ref, block_ref, wide_ref, out_ref):
    tiles = (out_ref.shape[0] - 8) // HD
    totals = [so_far_ref[t * HD : (t + 1) * HD, :] for t in range(tiles)]
    known = so_far_ref[tiles * HD :, :]
    sums = [known[t : t + 1] for t in range(tiles)]
    add_states(totals, sums, wanted(own_ref, tiles), (block_ref,), tiles)
    for t in range(tiles):
        wide_ref[t * HD : (t + 1) * HD, :] = totals[t]
        out_ref[t * HD : (t + 1) * HD, :] = totals[t].astype(BF16)
    tail = tail_rows(sums, [])
    wide_ref[tiles * HD :, :] = tail
    out_ref[tiles * HD :, :] = tail.astype(BF16)


def attend(q_refs, state_ref, out_ref, tiles):
    width, rows = out_ref.shape
    per_tile = rows // tiles
    first = q_refs[0].shape[1]
    exact = state_ref.dtype == F32
    tail = state_ref[tiles * HD :, :].astype(F32)
    for t in range(tiles):
        span = slice(t * per_tile, (t + 1) * per_tile)
        for start, size in head_blocks(width):
            lanes = slice(start, start + size)
            mask = same_head(size, size)
            state = state_ref[t * HD : (t + 1) * HD, lanes].astype(F32)
            state = jnp.concatenate([state] * (size // HD), axis=0)
            heads = size // HD
            parts = [jnp.where(mask, state, 0.0)]
            if exact:
                parts.append(parts[0] - parts[0].astype(BF16).astype(F32))
            row = lax.broadcasted_iota(jnp.int32, (8, size), 0)
            head = lax.broadcasted_iota(jnp.int32, (8, size), 1) // HD
            sums = jnp.where(row < 4, tail[t : t + 1, lanes], tail[tiles + t : tiles + t + 1, lanes])
            parts.append(jnp.where(row % 4 == head, sums, 0.0))
            left = jnp.concatenate(parts, axis=0).astype(BF16)
            both = lax.dot_general(
                left,
                q_refs[0][span, lanes] if start < first else q_refs[1][span, start - first : start - first + size],
                (((1,), (1,)), ((), ())), preferred_element_type=F32,
            )
            numer = both[:size]
            if exact:
                numer += both[size : 2 * size]
            sums = both[-8:]
            inverse = 1.0 / (sums[:4] + sums[4:] + 1e-06)
            inverse = jnp.concatenate(
                [jnp.broadcast_to(inverse[j : j + 1], (HD, per_tile)) for j in range(heads)], axis=0
            )
            out_ref[start : start + size, span] = (numer * inverse).astype(BF16)


def fetch_weights(p, width, w_refs, w_scr, sem):
    mine = lax.axis_index("rep")
    subs = w_refs[0].shape[1] // width
    for source, ref in enumerate(w_refs):
        @pl.when((p // subs == mine) == (source == 0))
        def _():
            pltpu.make_async_copy(ref, w_scr, sem).start()

    def finish():
        pltpu.make_async_copy(w_refs[0], w_scr, sem).wait()
        weights = w_scr[...]
        chosen = weights[:, :width]
        for s in range(1, subs):
            chosen = jnp.where(p % subs == s, weights[:, s * width : (s + 1) * width], chosen)
        return chosen

    return finish


def fifth_kernel(
    img_ref, qa_ref, qb_ref, state_ref, w0_ref, w1_ref, x_ref, mods_ref, base_ref, gate_ref,
    attn_scr, w_scr, x_scr, gates_scr, img_scr, sems,
):
    m = lax.axis_index("mp")
    cols, rows = base_ref.shape
    tiles = img_ref.shape[0]
    per_tile = rows // tiles
    finish = fetch_weights(m, attn_scr.shape[0], (w0_ref, w1_ref), w_scr, sems.at[0])
    copies = [
        pltpu.make_async_copy(img_ref, img_scr, sems.at[1]),
        pltpu.make_async_copy(x_ref.at[pl.ds(m * cols, cols), :], x_scr, sems.at[2]),
        pltpu.make_async_copy(mods_ref, gates_scr, sems.at[3]),
    ]
    for copy in copies:
        copy.start()
    attend((qa_ref, qb_ref), state_ref, attn_scr, tiles)
    weights = finish()
    for copy in copies:
        copy.wait()
    total = jnp.dot(weights, attn_scr[...], preferred_element_type=F32)
    for t in range(tiles):
        gates = gates_scr[img_scr[t]][2:3]
        gate = gates[:, :cols]
        for p in range(1, gates.shape[1] // cols):
            gate = jnp.where(m == p, gates[:, p * cols : (p + 1) * cols], gate)
        for start in range(0, cols, 128):
            size = min(128, cols - start)
            column = jnp.broadcast_to(gate[:, start : start + size], (128, size)).T
            gate_ref[start : start + size, t * 128 : (t + 1) * 128] = column
            for left in range(t * per_tile, (t + 1) * per_tile, 128):
                piece = (slice(start, start + size), slice(left, left + 128))
                base_ref[piece] = x_scr[piece].astype(F32) + column * total[piece]


def sixth_kernel(others, mp, tiles, *refs):
    qa_refs, qb_refs, state_refs = (refs[i * others : (i + 1) * others] for i in range(3))
    w0_ref, w1_ref, base_ref, gate_ref, out_ref, attn_scr, out_scr, sems = refs[3 * others :]
    m, mine = lax.axis_index("mp"), lax.axis_index("rep")
    cols, rows = out_ref.shape
    per_tile = rows // tiles
    width = attn_scr.shape[0]
    subs = w0_ref.shape[1] // width
    for index in range(others):
        attend((qa_refs[index], qb_refs[index]), state_refs[index], attn_scr, tiles)
        p = lax.rem(m + mp - 1 - index, mp)
        last = index == others - 1
        for source, ref in enumerate((w0_ref, w1_ref)):
            for s in range(subs):
                here = jnp.logical_and((p // subs == mine) == (source == 0), p % subs == s)

                @pl.when(here)
                def _(ref=ref, s=s, last=last):
                    for number, (start, size) in enumerate(pieces(cols)):
                        span = slice(start, start + size)
                        part = jnp.dot(
                            ref[span, s * width : (s + 1) * width], attn_scr[...],
                            preferred_element_type=F32,
                        )
                        for t in range(tiles):
                            column = gate_ref[span, t * 128 : (t + 1) * 128]
                            for left in range(t * per_tile, (t + 1) * per_tile, 128):
                                lanes = slice(left, left + 128)
                                value = base_ref[span, lanes] + column * part[:, lanes]
                                if last:
                                    out_scr[span, lanes] = value.astype(BF16)
                                else:
                                    base_ref[span, lanes] = value
                        if last:
                            pltpu.make_async_copy(
                                out_scr.at[span], out_ref.at[span], sems.at[number]
                            ).start()
    for number, (start, size) in enumerate(pieces(cols)):
        span = slice(start, start + size)
        pltpu.make_async_copy(out_scr.at[span], out_ref.at[span], sems.at[number]).wait()


def pieces(cols):
    unit = cols // 16 // 4 * 16
    return [(0, cols - 2 * unit), (cols - 2 * unit, unit), (cols - unit, unit)]


def seq_order(seq):
    return [*range((seq + 1) // 2, seq), *range(1, (seq + 1) // 2)]


def body(tokens, slot_image, modulation, w_qkv, w_out, *, seq, mp):
    rows, depth = tokens.shape
    tiles = slot_image.shape[0]
    half, _, width = w_qkv.shape
    heads_half, cols = w_out.shape
    swap = [(0, 1), (1, 0)]
    in_hbm = functools.partial(pltpu.with_memory_space_constraint, memory_space=pltpu.HBM)
    shape = jax.ShapeDtypeStruct
    x = in_hbm(tokens.T)
    w = in_hbm(jnp.transpose(w_qkv, (1, 0, 2)))
    wo = w_out.T
    dma = pltpu.SemaphoreType.DMA

    def shift(value, axis, size, by):
        return lax.ppermute(value, axis, [(i, (i + by) % size) for i in range(size)])

    def swap_seq(value, d):
        if seq & (seq - 1):
            return shift(value, "seq", seq, d)
        return lax.ppermute(value, "seq", [(i, i ^ d) for i in range(seq)])

    def across(value):
        return lax.ppermute(value, "rep", swap)

    lead = min(384, -(-width // 256) * 128)
    cuts = [(0, lead), (lead, width - lead)]
    kv_shapes, kv_spans = [], []
    for out, (start, size) in enumerate(cuts):
        joined = size % 128 == 0
        kv_shapes.append((1, half, 2 * size) if joined else (2, half, size))
        for c in range(2):
            kv_spans.append((out, 1 + c, start, size, 0 if joined else c, c * size if joined else 0))
    part_shapes = [shape((a, rows, c), F32) for a, _, c in kv_shapes]

    split = rows // 256 * 128

    def norm(begin, end, inputs, spans, loaded, before=(), known=()):
        spaces = [HB, VM, VM, HB] if begin else [HB] * 4
        scratch = [
            pltpu.SMEM((tiles,), jnp.int32), pltpu.VMEM((tiles, 8, half), F32),
            dma((3 + (end - begin) // 128 + len(spans),)),
        ]
        if not begin:
            scratch += [pltpu.VMEM((depth, end), BF16), pltpu.VMEM(modulation.shape, F32)]
        return call(
            functools.partial(norm_kernel, begin, end, spans, len(loaded)),
            [shape((rows, half), BF16)] * 2 + [shape(l, BF16) for l in loaded]
            + ([shape((1, split, lead), F32), *part_shapes] if known else []),
            spaces + [VM] * (len(before) + len(known)), scratch=scratch,
            aliases={4 + i: i for i in range(len(before))}, nbytes=4 * MIB,
        )(*inputs, w, *before, *known)

    own, other, wa, *kv, x_last = norm(
        0, split, (in_hbm(slot_image), x, in_hbm(modulation)),
        [(0, 0, 0, lead, 0, 0)] + [(1 + out, *rest) for out, *rest in kv_spans],
        [(1, half, lead)] + kv_shapes + [(depth, rows - split)],
    )
    wa_theirs = across(wa)
    kv_theirs = [across(k) for k in kv]
    own, other, wb, qa_part, *part = norm(
        split, rows, (slot_image, x_last, modulation), [(0, 0, lead, width - lead, 0, 0)],
        [(1, half, width - lead)], (own, other), (wa, *kv),
    )
    wb_theirs = across(wb)

    def query(size, mine, theirs, begin, *known):
        return call(
            functools.partial(query_kernel, begin), shape((rows, size), BF16), [VM] * (4 + len(known)),
            flops=2 * rows * depth * size, nbytes=3 * MIB,
        )(own, other, mine, theirs, *known)

    qa = query(lead, wa[0], wa_theirs[0], split, qa_part)
    qa_theirs = [shift(qa, "mp", mp, d) for d in range(1, mp)]
    part = call(
        functools.partial(part_kernel, split), part_shapes, [VM] * 6,
        aliases={4: 0, 5: 1}, flops=2 * rows * half * width, nbytes=4 * MIB,
    )(own, *kv, qa, *part)
    block = (state_rows(tiles), width)
    state = ()
    for i, (start, size) in enumerate(cuts):
        state = (call(
            functools.partial(second_kernel, start), shape(block, BF16),
            [HB] + [VM] * (3 + len(state)), aliases={4: 0} if state else None,
            scratch=[pltpu.VMEM((rows, size), BF16)] * 2 + [pltpu.SMEM((tiles,), jnp.int32), dma],
            flops=2 * rows * half * 2 * size, nbytes=6 * MIB,
        )(slot_image, other, kv_theirs[i], part[i], *state),)
    state = state[0]
    near = [state] + [swap_seq(state, d) for d in seq_order(seq)]
    qb = query(width - lead, wb[0], wb_theirs[0], 0)
    qb_theirs = [shift(qb, "mp", mp, d) for d in range(1, mp)]
    wo_theirs = across(wo)
    far = [across(b) for b in near]
    so_far = call(sum_kernel, shape(block, F32), [VM] * (2 * seq - 1), nbytes=MIB)(*near, *far[:-1])
    wide, final = call(
        last_kernel, [shape(block, F32), shape(block, BF16)], [VM] * 3, nbytes=MIB
    )(near[0], so_far, far[-1])
    finals = [shift(final, "mp", mp, d) for d in range(1, mp)]
    base, gate = call(
        fifth_kernel, [shape((cols, rows), F32), shape((cols, tiles * 128), F32)],
        [HB, VM, VM, VM, HB, HB, HB, HB],
        scratch=[
            pltpu.VMEM((width, rows), BF16), pltpu.VMEM((cols, heads_half), BF16), pltpu.VMEM((cols, rows), BF16),
            pltpu.VMEM(modulation.shape, F32), pltpu.SMEM((tiles,), jnp.int32), dma((4,)),
        ],
        flops=2 * rows * width * cols, nbytes=4 * MIB,
    )(slot_image, qa, qb, wide, wo, wo_theirs, x, modulation)
    out = call(
        functools.partial(sixth_kernel, mp - 1, mp, tiles), shape((cols, rows), BF16),
        [VM] * (3 * (mp - 1) + 4), out_specs=HB,
        scratch=[pltpu.VMEM((width, rows), BF16), pltpu.VMEM((cols, rows), BF16), dma((3,))],
        flops=2 * rows * width * cols, nbytes=4 * MIB,
    )(*qa_theirs, *qb_theirs, *finals, wo, wo_theirs, base, gate)
    return out.T


def solution(mesh):
    sizes = dict(mesh.shape)

    def step(*args):
        return body(*args, seq=sizes["seq"], mp=sizes["mp"])

    return jax.shard_map(
        step,
        mesh=mesh,
        in_specs=(
            P(("groups", "seq", "rep"), None),
            P(("groups", "seq", "rep")),
            P("groups", None, None),
            P("rep", None, "mp"),
            P("rep", "mp"),
        ),
        out_specs=P(("groups", "seq", "rep"), "mp"),
        check_vma=False,
    )
```
